32 devices in a mesh: groups: 2 (over y), seq: 4 (over z), tensor: 2 (over x), pipe: 2 (over core).
Axes of the slice: x: 2, y: 2, z: 4, core: 2. Of those that a mesh axis runs over, the one named last changes fastest.
Arguments:
- layer_input: bfloat16 [3072, 8192], P(('groups', 'seq'), ('tensor', 'pipe')), parts along dimension 0, may hold values from -6 to 6
- out_grad: bfloat16 [3072, 1024], P(('groups', 'seq')), parts along dimension 0, may hold values from -6 to 6
- value_weight: bfloat16 [1024, 8192], P('seq', ('tensor', 'pipe')), may hold values from -0.1875 to 0.1875
- adapter_down: bfloat16 [4, 64, 8192], P('seq', None, ('tensor', 'pipe')), may hold values from -0.0625 to 0.0625
- adapter_up: bfloat16 [4, 64, 1024], P('seq', None, ('tensor', 'pipe')), may hold values from -0.1875 to 0.1875
- block_tenant: int32 [24, 1], P(('groups', 'seq')), parts along dimension 0, may hold values from 0 to 3
- tenant_slot: int32 [4], replicated, may hold values from 0 to 3, each once
- forget_flag: int32 [3072], P(('groups', 'seq')), parts along dimension 0, may hold values 0 or 1
Outputs:
- layer_input_gradient: bfloat16 [3072, 8192], P(('groups', 'seq'), ('tensor', 'pipe')), parts along dimension 0
- down_grad: float32 [8, 64, 8192], P(('groups', 'seq'), None, ('tensor', 'pipe')), parts along dimension 0
- up_grad: float32 [8, 64, 1024], P(('groups', 'seq'), None, ('tensor', 'pipe')), parts along dimension 0
The draws below stay inside these ranges and needn't reach their ends.
There are 2 independent parts, one for each index of `groups`. The reference program is written for one: setup_inputs(seed, part) draws one part's arguments, and reference() takes and returns one part's arrays. A program takes and returns all parts, laid end to end along the dimension named above; an argument that names none is the same for every part. Nothing has to cross between parts.
Inputs may be any that keep to these rules, and one draw needn't show every extreme that they name: `block_tenant`: every tenant owns at least one block of 128 rows. A permutation: tenant t's adapter is row tenant_slot[t] of adapter_down and adapter_up.
All inputs are finite; a program needn't handle non-finite values. No bound on the sum of `forget_flag` on one device may be relied on, other than what follows from the above.
Results may differ from the reference program's by a relative error of at most 0.014.
Values may be sent and summed in bfloat16 or wider, within the bound.
No kernel may reach another device: no remote copies, remote signals or barrier semaphores. Data moves between devices by JAX's collectives and lax.ppermute only.
A program may use at most 64 MiB of HBM per device.

```python
import jax
import jax.numpy as jnp
from jax import lax

MODEL_WIDTH = 8192
DV = 1024
R = 64
BLOCK = 128
TOKEN_ROWS_LOCAL = 384
TOKENS = 1536
NBLOCKS = 12
TENANTS = 4
N_SEQ = 4


def set_ends(entries, rng, least, largest):
    extent = entries.shape
    index_at = [jax.random.randint(jax.random.fold_in(rng, axis), (), 0, extent[axis]) for axis in range(len(extent))]
    entries = entries.at[tuple(index_at)].set(least)
    longest = extent.index(max(extent))
    index_at[longest] = (index_at[longest] + 1) % extent[longest]
    return entries.at[tuple(index_at)].set(largest)


def steps_of(rng, shape, split, low, largest):
    def one(position, parts):
        draws = jax.random.uniform(jax.random.fold_in(jax.random.fold_in(rng, 6), position), (parts,), jnp.float32, low / len(split), largest / len(split))
        return jnp.repeat(jnp.exp(draws), shape[position] // parts).reshape((-1,) + (1,) * (len(shape) - position - 1))

    gain = one(*split[0])
    for cut in split[1:]:
        gain = gain * one(*cut)
    return gain


def distinct(key, rows, count, top, lift):
    order = jax.random.permutation(jax.random.fold_in(key, 1), count)
    boost = order
    for power in range(3):
        boost = boost * boost // count
    boost = boost * lift // count
    tickets = jax.random.randint(jax.random.fold_in(key, 2), (rows, count), 0, 4096) + boost
    sure = jax.random.permutation(jax.random.fold_in(key, 3), rows)[jnp.arange(count) % rows]
    tickets = jnp.where(jnp.arange(rows)[:, None] == sure[None, :], 1 << 14, tickets)
    priority = tickets * count + jnp.arange(count)
    return lax.top_k(priority.astype(jnp.int32), top)[1].astype(jnp.int32)


def noise(own_key, dims, deviation, reach, split=(), kind=jnp.bfloat16):
    factor_of = steps_of(own_key, dims, split, -0.22, 0.18) if split else 1.0
    result = jax.random.normal(own_key, dims, jnp.float32) * deviation * factor_of
    return jnp.minimum(jnp.maximum(result, -reach), reach).astype(kind)


def setup_inputs(seed: int = 0, part: int = 0) -> dict:
    seeds = jax.random.split(jax.random.key(seed), 9)
    part_keys = jax.random.split(jax.random.fold_in(seeds[8], part), 9)
    return {
        "layer_input": noise(part_keys[0], (TOKENS, MODEL_WIDTH), 1.0, 6.0, ((0, 4), (1, 4))),
        "out_grad": noise(part_keys[1], (TOKENS, DV), 1.0, 6.0, ((0, 4),)),
        "value_weight": noise(seeds[2], (DV, MODEL_WIDTH), DV ** -0.5, 0.1875, ((0, 4), (1, 4))),
        "adapter_down": noise(seeds[3], (TENANTS, R, MODEL_WIDTH), MODEL_WIDTH ** -0.5, 0.0625, ((0, 4), (2, 4))),
        "adapter_up": noise(seeds[4], (TENANTS, R, DV), DV ** -0.5, 0.1875, ((0, 4), (2, 4))),
        "block_tenant": distinct(part_keys[5], NBLOCKS, TENANTS, 1, 4096),
        "tenant_slot": jax.random.permutation(seeds[6], TENANTS).astype(jnp.int32),
        "forget_flag": set_ends((jax.random.randint(part_keys[7], (TOKENS,), 0, 2) < 1).astype(jnp.int32), jax.random.fold_in(part_keys[7], 1), 0, 1),
    }


adapter_scale_factor = 2.0


def reference(layer_input, out_grad, value_weight, adapter_down, adapter_up, block_tenant, tenant_slot, forget_flag):
    tenants = tenant_slot.shape[0]
    blocks_dev = TOKEN_ROWS_LOCAL // BLOCK
    highest_precision = lax.Precision.HIGHEST
    row_sign = (1 - 2 * forget_flag).astype(jnp.bfloat16)
    weighted = out_grad * row_sign[:, None]
    tenant_ids = jnp.arange(tenants, dtype=jnp.int32)
    block_slot = jnp.sum(jnp.where(block_tenant == tenant_ids[None, :], tenant_slot[None, :], 0), axis=1).astype(jnp.int32)
    inputs_dev = layer_input.reshape(N_SEQ, blocks_dev, BLOCK, MODEL_WIDTH)
    grads_dev = weighted.reshape(N_SEQ, blocks_dev, BLOCK, DV)
    slots_dev = block_slot.reshape(N_SEQ, blocks_dev)

    def per_device(carry, items):
        inputs, grads, slots = items
        selected_down_weight = jnp.take(adapter_down, slots, axis=0).astype(jnp.float32)
        selected_up_weight = jnp.take(adapter_up, slots, axis=0).astype(jnp.float32)
        inputs_f = inputs.astype(jnp.float32)
        output_gradient_float = grads.astype(jnp.float32)
        hidden = jnp.einsum("bnd,brd->bnr", inputs_f, selected_down_weight, precision=highest_precision)
        rank_projection = adapter_scale_factor * jnp.einsum("dck,dyk->dcy", output_gradient_float, selected_up_weight, precision=highest_precision)
        hidden_batch_rows = lax.optimization_barrier(hidden.astype(jnp.bfloat16)).astype(jnp.float32)
        rank_projection_batch = lax.optimization_barrier(rank_projection.astype(jnp.bfloat16)).astype(jnp.float32)
        frozen_input_gradient = jnp.dot(grads.reshape(TOKEN_ROWS_LOCAL, DV), value_weight, preferred_element_type=jnp.float32)
        adapter_input_gradient = jnp.einsum("tqi,tie->tqe", rank_projection_batch, selected_down_weight, precision=highest_precision).reshape(TOKEN_ROWS_LOCAL, MODEL_WIDTH)
        layer_input_gradient = (frozen_input_gradient + adapter_input_gradient).astype(jnp.bfloat16)
        part_down = jnp.einsum("bnd,bnr->brd", inputs_f, rank_projection_batch, precision=highest_precision)
        partial_up_weight = adapter_scale_factor * jnp.einsum("yxj,yxl->yjl", hidden_batch_rows, output_gradient_float, precision=highest_precision)
        select = (slots[:, None] == tenant_ids[None, :]).astype(jnp.float32)
        table_down = jnp.einsum("bs,brd->srd", select, part_down, precision=highest_precision)
        table_up = jnp.einsum("bs,brv->srv", select, partial_up_weight, precision=highest_precision)
        table_down = lax.optimization_barrier(table_down.astype(jnp.bfloat16)).astype(jnp.float32)
        table_up = lax.optimization_barrier(table_up.astype(jnp.bfloat16)).astype(jnp.float32)
        return (carry[0] + table_down, carry[1] + table_up), layer_input_gradient

    initial = (jnp.zeros((tenants, R, MODEL_WIDTH), jnp.float32), jnp.zeros((tenants, R, DV), jnp.float32))
    sums, grads_rows = lax.scan(per_device, initial, (inputs_dev, grads_dev, slots_dev))
    return grads_rows.reshape(TOKENS, MODEL_WIDTH), sums[0], sums[1]
```

```python
import functools

import jax
import jax.numpy as jnp
from jax import lax
from jax.experimental import pallas as pl
from jax.experimental.pallas import tpu as pltpu
from jax.sharding import PartitionSpec as P

SCALE = 2.0
VMEM_LIMIT = 48 << 20
F32 = jnp.float32
BF16 = jnp.bfloat16


def project_kernel(slots, x_ref, w_ref, down_ref, up_ref, out_ref):
    blocks = slots.shape[0]
    rows = x_ref.shape[0] // blocks
    rank = down_ref.shape[1]
    contract = (((1,), (1,)), ((), ()))
    for b in range(blocks):
        s = slots[b]
        span = pl.ds(b * rows, rows)
        hidden = lax.dot_general(x_ref[span, :], down_ref[s], contract, preferred_element_type=F32)
        low = lax.dot_general(w_ref[span, :], up_ref[s], contract, preferred_element_type=F32)
        out_ref[span, :rank] = hidden.astype(BF16)
        out_ref[span, rank:] = low.astype(BF16)


def grads_kernel(slots, x_ref, w_ref, here_ref, there_ref, table_ref, low_ref, acc_ref):
    blocks = slots.shape[0]
    rows, width = x_ref.shape[0] // blocks, x_ref.shape[1]
    rank = low_ref.shape[1]
    contract = (((0,), (0,)), ((), ()))
    total = here_ref[...].astype(F32) + there_ref[...].astype(F32)
    hidden_b = total[:, :rank].astype(BF16)
    low_b = (SCALE * total[:, rank:]).astype(BF16)
    low_ref[...] = low_b
    acc_ref[...] = jnp.zeros_like(acc_ref)
    for b in range(blocks):
        s = slots[b]
        span = slice(b * rows, (b + 1) * rows)
        acc_ref[s, :, :width] += lax.dot_general(
            low_b[span], x_ref[span, :], contract, preferred_element_type=F32
        )
        acc_ref[s, :, width:] += SCALE * lax.dot_general(
            hidden_b[span], w_ref[span, :], contract, preferred_element_type=F32
        )
    table_ref[...] = acc_ref[...].astype(BF16)


def product_kernel(count, scalars, *refs):
    low_ref, weighted_ref, down_ref, own_ref = refs[:4]
    pieces, out_ref = refs[4 : 4 + count], refs[-1]
    rows, depth = low_ref.shape[0], own_ref.shape[0]
    blocks = scalars.shape[0] - 1
    block_rows = rows // blocks
    total = jnp.dot(weighted_ref[:, :depth], own_ref[...], preferred_element_type=F32)
    for j, piece in enumerate(pieces):
        total += jnp.dot(
            weighted_ref[:, (j + 1) * depth : (j + 2) * depth],
            piece[...],
            preferred_element_type=F32,
        )
    for b in range(blocks):
        span = slice(b * block_rows, (b + 1) * block_rows)
        term = jnp.dot(low_ref[span, :], down_ref[scalars[b]], preferred_element_type=F32)
        out_ref[span, :] = (total[span] + term).astype(BF16)


def product(half, slots, low_b, weighted, gathered, own, pieces, width, into=None):
    rows, rank = low_b.shape
    tenants = gathered.shape[0]
    depth = own.shape[0]
    part = width // 2
    tile = min(512, part)
    tiles = part // tile
    scalars = jnp.concatenate([slots, half[None]])
    blocks = slots.shape[0]
    whole = lambda i, s: (0, 0)
    column = lambda i, s: (0, s[blocks] * tiles + i)
    specs = [
        pl.BlockSpec((rows, rank), whole),
        pl.BlockSpec(weighted.shape, whole),
        pl.BlockSpec((tenants, rank, tile), lambda i, s: (0, 0, s[blocks] * tiles + i)),
        pl.BlockSpec((depth, tile), column),
    ] + [pl.BlockSpec((depth, tile), lambda i, s: (0, i)) for _ in pieces]
    operands = [low_b, weighted, gathered, own, *pieces]
    aliases = {}
    if into is not None:
        specs.append(pl.BlockSpec(memory_space=pl.ANY))
        operands.append(into)
        aliases = {len(operands): 0}
    return pl.pallas_call(
        functools.partial(product_kernel, len(pieces)),
        out_shape=jax.ShapeDtypeStruct((rows, width), BF16),
        grid_spec=pltpu.PrefetchScalarGridSpec(
            num_scalar_prefetch=1,
            grid=(tiles,),
            in_specs=specs,
            out_specs=pl.BlockSpec((rows, tile), column),
        ),
        input_output_aliases=aliases,
        compiler_params=pltpu.CompilerParams(vmem_limit_bytes=VMEM_LIMIT),
        cost_estimate=pl.CostEstimate(
            flops=2 * rows * part * (weighted.shape[1] + rank),
            bytes_accessed=2 * (part * (weighted.shape[1] + tenants * rank + rows)),
            transcendentals=0,
        ),
        name="product",
    )(scalars, *operands)


def project(slots, x, own_cols, gathered):
    rows, width = x.shape
    tenants, rank = gathered.shape[:2]
    slab = own_cols.shape[1]
    return pl.pallas_call(
        project_kernel,
        out_shape=jax.ShapeDtypeStruct((rows, 2 * rank), BF16),
        grid_spec=pltpu.PrefetchScalarGridSpec(
            num_scalar_prefetch=1,
            grid=(1,),
            in_specs=[
                pl.BlockSpec((rows, width), lambda i, s: (0, 0)),
                pl.BlockSpec((rows, slab), lambda i, s: (0, 0)),
                pl.BlockSpec((tenants, rank, width), lambda i, s: (0, 0, 0)),
                pl.BlockSpec((tenants, rank, slab), lambda i, s: (0, 0, width // slab)),
            ],
            out_specs=pl.BlockSpec((rows, 2 * rank), lambda i, s: (0, 0)),
        ),
        compiler_params=pltpu.CompilerParams(vmem_limit_bytes=VMEM_LIMIT),
        cost_estimate=pl.CostEstimate(
            flops=2 * rows * rank * (width + slab),
            bytes_accessed=2 * (rows + tenants * rank) * (width + slab),
            transcendentals=0,
        ),
        name="project",
    )(slots, x, own_cols, gathered, gathered)


def adapter_grads(slots, x, own_cols, here, there, tenants):
    rows, width = x.shape
    rank = here.shape[1] // 2
    slab = own_cols.shape[1]
    return pl.pallas_call(
        grads_kernel,
        out_shape=(
            jax.ShapeDtypeStruct((tenants, rank, width + slab), BF16),
            jax.ShapeDtypeStruct((rows, rank), BF16),
        ),
        grid_spec=pltpu.PrefetchScalarGridSpec(
            num_scalar_prefetch=1,
            grid=(1,),
            in_specs=[
                pl.BlockSpec((rows, width), lambda i, s: (0, 0)),
                pl.BlockSpec((rows, slab), lambda i, s: (0, 0)),
                pl.BlockSpec((rows, 2 * rank), lambda i, s: (0, 0)),
                pl.BlockSpec((rows, 2 * rank), lambda i, s: (0, 0)),
            ],
            out_specs=[
                pl.BlockSpec((tenants, rank, width + slab), lambda i, s: (0, 0, 0)),
                pl.BlockSpec((rows, rank), lambda i, s: (0, 0)),
            ],
            scratch_shapes=[pltpu.VMEM((tenants, rank, width + slab), F32)],
        ),
        compiler_params=pltpu.CompilerParams(vmem_limit_bytes=VMEM_LIMIT),
        cost_estimate=pl.CostEstimate(
            flops=2 * rows * rank * (width + slab),
            bytes_accessed=2 * (rows + tenants * rank) * (width + slab),
            transcendentals=0,
        ),
        name="adapter_grads",
    )(slots, x, own_cols, here, there)


def arrivals(n):
    table = []
    for i in range(n):
        order = []
        for k in range(1, n):
            if i >= k:
                order.append(("up", k))
            if i + k < n:
                order.append(("down", k))
        table.append(order)
    return table


def pick(me, choices):
    out = choices[0]
    for i in range(1, len(choices)):
        if any(choices[i] is c for c in choices[:i]) and choices[i] is choices[i - 1]:
            continue
        out = jnp.where(me >= i, choices[i], out)
    return out


def gather_line(piece, n):
    me = lax.axis_index("seq")
    got = {}
    up = down = piece
    for k in range(1, n):
        up_pairs = [(i, i + 1) for i in range(k - 1, n - 1)]
        down_pairs = [(i + 1, i) for i in range(n - k)]
        if {a for a, _ in up_pairs} & {a for a, _ in down_pairs}:
            up = lax.ppermute(up, "seq", up_pairs)
            down = lax.ppermute(down, "seq", down_pairs)
        else:
            both = jnp.where(me >= k - 1, up, down)
            up = down = lax.ppermute(both, "seq", up_pairs + down_pairs)
        got["up", k], got["down", k] = up, down
    table = arrivals(n)
    pieces, owners = [], []
    for j in range(n - 1):
        pieces.append(pick(me, [got[table[i][j]] for i in range(n)]))
        source = [i - k if d == "up" else i + k for i in range(n) for d, k in [table[i][j]]]
        owners.append(jnp.asarray(source, jnp.int32)[me])
    return pieces, owners


def per_device(
    sizes,
    layer_input,
    out_grad,
    value_weight,
    adapter_down,
    adapter_up,
    block_tenant,
    tenant_slot,
    forget_flag,
):
    n, groups = sizes
    token_rows, width = layer_input.shape
    owned, rank, _ = adapter_down.shape
    slab = adapter_up.shape[2]
    tenants = tenant_slot.shape[0]
    depth = value_weight.shape[0]
    swap = lambda axis: functools.partial(lax.ppermute, axis_name=axis, perm=[(0, 1), (1, 0)])

    adapters = jnp.concatenate([adapter_down, adapter_up], axis=2)
    gathered = lax.all_gather(adapters, "seq", axis=0, tiled=True)

    group = lax.axis_index("groups").astype(jnp.int32)
    piece = lax.dynamic_slice_in_dim(value_weight, group * (width // 2), width // 2, 1)
    mine, owners = gather_line(piece, n)
    other = [swap("groups")(p) for p in mine]

    row_sign = (1 - 2 * forget_flag).astype(BF16)
    weighted = out_grad * row_sign[:, None]
    tenant_ids = jnp.arange(tenants, dtype=jnp.int32)
    slots = jnp.sum(
        jnp.where(block_tenant == tenant_ids[None, :], tenant_slot[None, :], 0), axis=1
    ).astype(jnp.int32)
    slab_index = lax.axis_index(("tensor", "pipe"))
    own_cols = lax.dynamic_slice_in_dim(weighted, slab_index * slab, slab, 1)
    me = lax.axis_index("seq")
    ordered = jnp.concatenate(
        [lax.dynamic_slice_in_dim(weighted, o * depth, depth, 1) for o in [me, *owners]], axis=1
    )

    part = project(slots, layer_input, own_cols, gathered)
    here = part
    axes = [a for a in ("pipe", "tensor")]
    for axis in axes[:-1]:
        here = (here.astype(F32) + line_sum_rest(here, axis, sizes)).astype(BF16)
    there = line_sum_rest(here, axes[-1], sizes).astype(BF16)
    table, low_b = adapter_grads(slots, layer_input, own_cols, here, there, tenants)
    got = lax.all_to_all(table, "seq", split_axis=0, concat_axis=0, tiled=True)
    total = jnp.sum(got.astype(F32).reshape(n, owned, rank, width + slab), axis=0)
    down_grad, up_grad = total[:, :, :width], total[:, :, width:]

    half = product(group, slots, low_b, ordered, gathered, value_weight, mine, width)
    full = product(1 - group, slots, low_b, ordered, gathered, value_weight, other, width, half)
    return full, down_grad, up_grad


def line_sum_rest(value, axis, sizes):
    size = lax.axis_size(axis)
    rest = 0.0
    for d in range(1, size):
        rest = rest + lax.ppermute(
            value, axis, [(i, (i + d) % size) for i in range(size)]
        ).astype(F32)
    return rest


def solution(mesh):
    sizes = (mesh.shape["seq"], mesh.shape["groups"])
    return jax.shard_map(
        functools.partial(per_device, sizes),
        mesh=mesh,
        in_specs=(
            P(("groups", "seq"), ("tensor", "pipe")),
            P(("groups", "seq"), None),
            P("seq", ("tensor", "pipe")),
            P("seq", None, ("tensor", "pipe")),
            P("seq", None, ("tensor", "pipe")),
            P(("groups", "seq"), None),
            P(),
            P(("groups", "seq")),
        ),
        out_specs=(
            P(("groups", "seq"), ("tensor", "pipe")),
            P(("groups", "seq"), None, ("tensor", "pipe")),
            P(("groups", "seq"), None, ("tensor", "pipe")),
        ),
        check_vma=False,
    )
```

```python
import functools

import jax
import jax.numpy as jnp
from jax import lax
from jax.experimental import pallas as pl
from jax.experimental.pallas import tpu as pltpu
from jax.sharding import PartitionSpec as P

SCALE = 2.0
VMEM_LIMIT = 48 << 20
F32 = jnp.float32
BF16 = jnp.bfloat16


def project_kernel(blocks, scalars, x_ref, w_ref, mine_ref, other_ref, up_ref, out_ref):
    rows = x_ref.shape[0] // blocks
    rank, part = mine_ref.shape[1:]
    contract = (((1,), (1,)), ((), ()))

    def run(first, second):
        for b in range(blocks):
            s = scalars[b]
            span = slice(b * rows, (b + 1) * rows)
            hidden = lax.dot_general(
                x_ref[span, :part], first[s], contract, preferred_element_type=F32
            ) + lax.dot_general(
                x_ref[span, part:], second[s], contract, preferred_element_type=F32
            )
            low = lax.dot_general(w_ref[span, :], up_ref[s], contract, preferred_element_type=F32)
            out_ref[span, :rank] = hidden.astype(BF16)
            out_ref[span, rank:] = low.astype(BF16)

    @pl.when(scalars[blocks] == 0)
    def _():
        run(mine_ref, other_ref)

    @pl.when(scalars[blocks] != 0)
    def _():
        run(other_ref, mine_ref)


def grads_kernel(slots, x_ref, w_ref, here_ref, there_ref, table_ref, low_ref, acc_ref):
    blocks = slots.shape[0]
    rows, width = x_ref.shape[0] // blocks, x_ref.shape[1]
    rank = low_ref.shape[1]
    contract = (((0,), (0,)), ((), ()))
    total = here_ref[...].astype(F32) + there_ref[...].astype(F32)
    hidden_b = total[:, :rank].astype(BF16)
    low_b = (SCALE * total[:, rank:]).astype(BF16)
    low_ref[...] = low_b
    acc_ref[...] = jnp.zeros_like(acc_ref)
    for b in range(blocks):
        s = slots[b]
        span = slice(b * rows, (b + 1) * rows)
        acc_ref[s, :, :width] += lax.dot_general(
            low_b[span], x_ref[span, :], contract, preferred_element_type=F32
        )
        acc_ref[s, :, width:] += SCALE * lax.dot_general(
            hidden_b[span], w_ref[span, :], contract, preferred_element_type=F32
        )
    table_ref[...] = acc_ref[...].astype(BF16)


def product_kernel(count, blocks, scalars, *refs):
    low_ref, weighted_ref, down_ref, own_ref = refs[:4]
    pieces, out_ref, acc_ref = refs[4 : 4 + count], refs[-2], refs[-1]
    rows, depth = low_ref.shape[0], own_ref.shape[0]
    block_rows = rows // blocks
    for b in range(blocks):
        span = slice(b * block_rows, (b + 1) * block_rows)
        acc_ref[span, :] = jnp.dot(
            low_ref[span, :], down_ref[scalars[b]], preferred_element_type=F32
        ) + jnp.dot(weighted_ref[span, :depth], own_ref[...], preferred_element_type=F32)
    for j, piece in enumerate(pieces):

        @pl.when(scalars[blocks + 1 + j] > 0)
        def _(j=j, piece=piece):
            acc_ref[...] += jnp.dot(
                weighted_ref[:, (j + 1) * depth : (j + 2) * depth],
                piece[...],
                preferred_element_type=F32,
            )

    out_ref[...] = acc_ref[...].astype(BF16)


def product(half, slots, valid, low_b, weighted, down, own, pieces, width, into=None):
    rows, rank = low_b.shape
    tenants = down.shape[0]
    depth = own.shape[0]
    part = width // 2
    tile = min(512, part)
    tiles = part // tile
    blocks = slots.shape[0]
    scalars = jnp.concatenate([slots, half[None], valid])
    whole = lambda i, s: (0, 0)
    column = lambda i, s: (0, s[blocks] * tiles + i)
    specs = [
        pl.BlockSpec((rows, rank), whole),
        pl.BlockSpec(weighted.shape, whole),
        pl.BlockSpec((tenants, rank, tile), lambda i, s: (0, 0, i)),
        pl.BlockSpec((depth, tile), column),
    ] + [pl.BlockSpec((depth, tile), lambda i, s: (0, i)) for _ in pieces]
    operands = [low_b, weighted, down, own, *pieces]
    aliases = {}
    if into is not None:
        specs.append(pl.BlockSpec(memory_space=pl.ANY))
        operands.append(into)
        aliases = {len(operands): 0}
    return pl.pallas_call(
        functools.partial(product_kernel, len(pieces), blocks),
        out_shape=jax.ShapeDtypeStruct((rows, width), BF16),
        grid_spec=pltpu.PrefetchScalarGridSpec(
            num_scalar_prefetch=1,
            grid=(tiles,),
            in_specs=specs,
            out_specs=pl.BlockSpec((rows, tile), column),
            scratch_shapes=[pltpu.VMEM((rows, tile), F32)],
        ),
        input_output_aliases=aliases,
        compiler_params=pltpu.CompilerParams(vmem_limit_bytes=VMEM_LIMIT),
        cost_estimate=pl.CostEstimate(
            flops=2 * rows * part * (weighted.shape[1] + rank),
            bytes_accessed=2 * (part * (weighted.shape[1] + tenants * rank + rows)),
            transcendentals=0,
        ),
        name="product",
    )(scalars, *operands)


def project(group, slots, x, own_cols, received, other):
    rows, width = x.shape
    tenants, rank, part = other.shape
    slab = own_cols.shape[1]
    return pl.pallas_call(
        functools.partial(project_kernel, slots.shape[0]),
        out_shape=jax.ShapeDtypeStruct((rows, 2 * rank), BF16),
        grid_spec=pltpu.PrefetchScalarGridSpec(
            num_scalar_prefetch=1,
            grid=(1,),
            in_specs=[
                pl.BlockSpec((rows, width), lambda i, s: (0, 0)),
                pl.BlockSpec((rows, slab), lambda i, s: (0, 0)),
                pl.BlockSpec((tenants, rank, part), lambda i, s: (0, 0, 0)),
                pl.BlockSpec((tenants, rank, part), lambda i, s: (0, 0, 0)),
                pl.BlockSpec((tenants, rank, slab), lambda i, s: (0, 0, part // slab)),
            ],
            out_specs=pl.BlockSpec((rows, 2 * rank), lambda i, s: (0, 0)),
        ),
        compiler_params=pltpu.CompilerParams(vmem_limit_bytes=VMEM_LIMIT),
        cost_estimate=pl.CostEstimate(
            flops=2 * rows * rank * (width + slab),
            bytes_accessed=2 * (rows + tenants * rank) * (width + slab),
            transcendentals=0,
        ),
        name="project",
    )(jnp.concatenate([slots, group[None]]), x, own_cols, received, other, received)


def adapter_grads(slots, x, own_cols, here, there, tenants):
    rows, width = x.shape
    rank = here.shape[1] // 2
    slab = own_cols.shape[1]
    return pl.pallas_call(
        grads_kernel,
        out_shape=(
            jax.ShapeDtypeStruct((tenants, rank, width + slab), BF16),
            jax.ShapeDtypeStruct((rows, rank), BF16),
        ),
        grid_spec=pltpu.PrefetchScalarGridSpec(
            num_scalar_prefetch=1,
            grid=(1,),
            in_specs=[
                pl.BlockSpec((rows, width), lambda i, s: (0, 0)),
                pl.BlockSpec((rows, slab), lambda i, s: (0, 0)),
                pl.BlockSpec((rows, 2 * rank), lambda i, s: (0, 0)),
                pl.BlockSpec((rows, 2 * rank), lambda i, s: (0, 0)),
            ],
            out_specs=[
                pl.BlockSpec((tenants, rank, width + slab), lambda i, s: (0, 0, 0)),
                pl.BlockSpec((rows, rank), lambda i, s: (0, 0)),
            ],
            scratch_shapes=[pltpu.VMEM((tenants, rank, width + slab), F32)],
        ),
        compiler_params=pltpu.CompilerParams(vmem_limit_bytes=VMEM_LIMIT),
        cost_estimate=pl.CostEstimate(
            flops=2 * rows * rank * (width + slab),
            bytes_accessed=2 * (rows + tenants * rank) * (width + slab),
            transcendentals=0,
        ),
        name="adapter_grads",
    )(slots, x, own_cols, here, there)


def sum_kernel(got_ref, down_ref, up_ref):
    width = down_ref.shape[2]
    total = got_ref[0].astype(F32)
    for k in range(1, got_ref.shape[0]):
        total += got_ref[k].astype(F32)
    down_ref[0] = total[:, :width]
    up_ref[0] = total[:, width:]


def owner_sums(got, width):
    _, rank, both = got.shape
    return pl.pallas_call(
        sum_kernel,
        out_shape=(
            jax.ShapeDtypeStruct((1, rank, width), F32),
            jax.ShapeDtypeStruct((1, rank, both - width), F32),
        ),
        compiler_params=pltpu.CompilerParams(vmem_limit_bytes=VMEM_LIMIT),
        cost_estimate=pl.CostEstimate(
            flops=got.size, bytes_accessed=2 * got.size, transcendentals=0
        ),
        name="owner_sums",
    )(got)


def gather_line(piece, n, groups):
    me = lax.axis_index("seq").astype(jnp.int32)
    mine, other, owner, valid = [], [], [], []
    up = down = piece

    def keep(value, pairs, source):
        targets = [b for _, b in pairs]
        swaps = [
            (g * n + t, (groups - 1 - g) * n + t) for g in range(groups) for t in targets
        ]
        mine.append(value)
        other.append(lax.ppermute(value, ("groups", "seq"), swaps))
        low, high = min(targets), max(targets)
        has = (me >= low) & (me <= high)
        if len(targets) < high - low + 1:
            gap = [t for t in range(low, high) if t not in targets]
            has = has & ((me < gap[0]) | (me > gap[-1]))
        owner.append(jnp.where(has, source, 0))
        valid.append(has.astype(jnp.int32))

    for k in range(1, n):
        up_pairs = [(i, i + 1) for i in range(k - 1, n - 1)]
        down_pairs = [(i + 1, i) for i in range(n - k)]
        if {a for a, _ in up_pairs} & {a for a, _ in down_pairs}:
            up = lax.ppermute(up, "seq", up_pairs)
            down = lax.ppermute(down, "seq", down_pairs)
            keep(up, up_pairs, me - k)
            keep(down, down_pairs, me + k)
        else:
            both = jnp.where(me >= k - 1, up, down)
            up = down = lax.ppermute(both, "seq", up_pairs + down_pairs)
            keep(up, up_pairs + down_pairs, jnp.where(me >= k, me - k, me + k))
    return mine, other, owner, jnp.stack(valid)


def per_device(
    sizes,
    layer_input,
    out_grad,
    value_weight,
    adapter_down,
    adapter_up,
    block_tenant,
    tenant_slot,
    forget_flag,
):
    n, groups = sizes
    token_rows, width = layer_input.shape
    rank = adapter_down.shape[1]
    slab = adapter_up.shape[2]
    tenants = tenant_slot.shape[0]
    depth = value_weight.shape[0]
    swap = lambda axis: functools.partial(lax.ppermute, axis_name=axis, perm=[(0, 1), (1, 0)])

    half = width // 2
    group = lax.axis_index("groups").astype(jnp.int32)
    down_half = lax.dynamic_slice_in_dim(adapter_down, group * half, half, 2)
    adapters = jnp.concatenate([down_half, adapter_up], axis=2)
    received = lax.all_to_all(
        jnp.broadcast_to(adapters, (n,) + adapters.shape).reshape(tenants, rank, half + slab),
        "seq",
        split_axis=0,
        concat_axis=0,
        tiled=True,
    )
    swapped = swap("groups")(received[:, :, :half])

    piece = lax.dynamic_slice_in_dim(value_weight, group * half, half, 1)
    mine, other, owners, valid = gather_line(piece, n, groups)

    row_sign = (1 - 2 * forget_flag).astype(BF16)
    weighted = out_grad * row_sign[:, None]
    tenant_ids = jnp.arange(tenants, dtype=jnp.int32)
    slots = jnp.sum(
        jnp.where(block_tenant == tenant_ids[None, :], tenant_slot[None, :], 0), axis=1
    ).astype(jnp.int32)
    slab_index = lax.axis_index(("tensor", "pipe"))
    own_cols = lax.dynamic_slice_in_dim(weighted, slab_index * slab, slab, 1)
    me = lax.axis_index("seq")
    ordered = jnp.concatenate(
        [lax.dynamic_slice_in_dim(weighted, o * depth, depth, 1) for o in [me, *owners]], axis=1
    )

    part = project(group, slots, layer_input, own_cols, received, swapped)
    here = part
    axes = [a for a in ("pipe", "tensor")]
    for axis in axes[:-1]:
        here = (here.astype(F32) + line_sum_rest(here, axis, sizes)).astype(BF16)
    there = line_sum_rest(here, axes[-1], sizes).astype(BF16)
    table, low_b = adapter_grads(slots, layer_input, own_cols, here, there, tenants)
    got = lax.all_to_all(table, "seq", split_axis=0, concat_axis=0, tiled=True)
    down_grad, up_grad = owner_sums(got, width)

    first = product(
        group, slots, valid, low_b, ordered, received, value_weight, mine, width
    )
    full = product(
        1 - group, slots, valid, low_b, ordered, swapped, value_weight, other, width, first
    )
    return full, down_grad, up_grad


def line_sum_rest(value, axis, sizes):
    size = lax.axis_size(axis)
    rest = 0.0
    for d in range(1, size):
        rest = rest + lax.ppermute(
            value, axis, [(i, (i + d) % size) for i in range(size)]
        ).astype(F32)
    return rest


def solution(mesh):
    sizes = (mesh.shape["seq"], mesh.shape["groups"])
    return jax.shard_map(
        functools.partial(per_device, sizes),
        mesh=mesh,
        in_specs=(
            P(("groups", "seq"), ("tensor", "pipe")),
            P(("groups", "seq"), None),
            P("seq", ("tensor", "pipe")),
            P("seq", None, ("tensor", "pipe")),
            P("seq", None, ("tensor", "pipe")),
            P(("groups", "seq"), None),
            P(),
            P(("groups", "seq")),
        ),
        out_specs=(
            P(("groups", "seq"), ("tensor", "pipe")),
            P(("groups", "seq"), None, ("tensor", "pipe")),
            P(("groups", "seq"), None, ("tensor", "pipe")),
        ),
        check_vma=False,
    )
```

```python
import functools

import jax
import jax.numpy as jnp
from jax import lax
from jax.experimental import pallas as pl
from jax.experimental.pallas import tpu as pltpu
from jax.sharding import PartitionSpec as P

SCALE = 2.0
VMEM_LIMIT = 48 << 20
F32 = jnp.float32
BF16 = jnp.bfloat16


def project_kernel(blocks, scalars, x_ref, w_ref, mine_ref, other_ref, up_ref, out_ref):
    rows = x_ref.shape[0] // blocks
    rank, part = mine_ref.shape[1:]
    contract = (((1,), (1,)), ((), ()))

    def run(first, second):
        for b in range(blocks):
            s = scalars[b]
            span = slice(b * rows, (b + 1) * rows)
            hidden = lax.dot_general(
                x_ref[span, :part], first[s], contract, preferred_element_type=F32
            ) + lax.dot_general(
                x_ref[span, part:], second[s], contract, preferred_element_type=F32
            )
            low = lax.dot_general(w_ref[span, :], up_ref[s], contract, preferred_element_type=F32)
            out_ref[span, :rank] = hidden.astype(BF16)
            out_ref[span, rank:] = low.astype(BF16)

    @pl.when(scalars[blocks] == 0)
    def _():
        run(mine_ref, other_ref)

    @pl.when(scalars[blocks] != 0)
    def _():
        run(other_ref, mine_ref)


def grads_kernel(blocks, slots, x_ref, w_ref, here_ref, there_ref, table_ref, low_ref, acc_ref):
    rows, width = x_ref.shape[0] // blocks, x_ref.shape[1]
    rank = low_ref.shape[1]
    contract = (((0,), (0,)), ((), ()))
    total = here_ref[...].astype(F32) + there_ref[...].astype(F32)
    hidden_b = total[:, :rank].astype(BF16)
    low_b = (SCALE * total[:, rank:]).astype(BF16)
    low_ref[...] = low_b
    acc_ref[...] = jnp.zeros_like(acc_ref)
    for b in range(blocks):
        s = slots[b]
        span = slice(b * rows, (b + 1) * rows)
        acc_ref[s, :, :width] += lax.dot_general(
            low_b[span], x_ref[span, :], contract, preferred_element_type=F32
        )
        acc_ref[s, :, width:] += SCALE * lax.dot_general(
            hidden_b[span], w_ref[span, :], contract, preferred_element_type=F32
        )
    table_ref[...] = acc_ref[...].astype(BF16)


def product_kernel(plan, scalars, *refs):
    count, blocks, opens, aligned = plan
    refs = list(refs)
    weighted_ref = refs.pop(0)
    acc_ref, out_ref = refs.pop(), refs.pop()
    if opens:
        low_ref, down_ref, own_ref = refs[:3]
        pieces = refs[3 : 3 + count]
        depth = own_ref.shape[0]
        block_rows = low_ref.shape[0] // blocks
        own = take_columns(weighted_ref, scalars[blocks + 1], 0, depth, aligned)
        acc_ref[...] = jnp.dot(own, own_ref[...], preferred_element_type=F32)
        for b in range(blocks):
            span = slice(b * block_rows, (b + 1) * block_rows)
            acc_ref[span, :] += jnp.dot(
                low_ref[span, :], down_ref[scalars[b]], preferred_element_type=F32
            )
    else:
        pieces = refs[1 : 1 + count]
        depth = pieces[0].shape[0]
        acc_ref[...] = refs[0][...]
    for j, piece in enumerate(pieces):
        owner = scalars[blocks + 2 + j]

        @pl.when(owner >= 0)
        def _(j=j, piece=piece, owner=owner):
            columns = take_columns(weighted_ref, owner, j + 1, depth, aligned)
            acc_ref[...] += jnp.dot(columns, piece[...], preferred_element_type=F32)

    out_ref[...] = acc_ref[...].astype(out_ref.dtype)


def take_columns(ref, owner, position, depth, aligned):
    if aligned:
        return ref[:, pl.ds(pl.multiple_of(owner * depth, 128), depth)]
    return ref[:, position * depth : (position + 1) * depth]


def product(half, slots, me, owners, weighted, pieces, start, width, into=None, partial=False):
    opens = isinstance(start, tuple)
    rows = weighted.shape[0]
    depth = pieces[0].shape[0]
    part = width // 2
    tile = min(512, part)
    tiles = part // tile
    blocks = slots.shape[0]
    aligned = depth % 128 == 0
    if not aligned:
        begins = [me] + [jnp.maximum(o, 0) for o in owners]
        weighted = jnp.concatenate(
            [lax.dynamic_slice_in_dim(weighted, o * depth, depth, 1) for o in begins], axis=1
        )
    scalars = jnp.stack([*slots, half, me, *owners])
    whole = lambda i, s: (0, 0)
    here = lambda i, s: (0, i)
    column = lambda i, s: (0, s[blocks] * tiles + i)
    specs = [pl.BlockSpec(weighted.shape, whole)]
    operands = [weighted]
    if opens:
        low_b, down, own = start
        specs += [
            pl.BlockSpec(low_b.shape, whole),
            pl.BlockSpec((*down.shape[:2], tile), lambda i, s: (0, 0, i)),
            pl.BlockSpec((depth, tile), column),
        ]
        operands += [low_b, down, own]
    else:
        specs.append(pl.BlockSpec((rows, tile), here))
        operands.append(start)
    specs += [pl.BlockSpec((depth, tile), here) for _ in pieces]
    operands += pieces
    aliases = {}
    if into is not None:
        specs.append(pl.BlockSpec(memory_space=pl.ANY))
        operands.append(into)
        aliases = {len(operands): 0}
    shape = jax.ShapeDtypeStruct((rows, part), F32) if partial else jax.ShapeDtypeStruct((rows, width), BF16)
    return pl.pallas_call(
        functools.partial(product_kernel, (len(pieces), blocks, opens, aligned)),
        out_shape=shape,
        grid_spec=pltpu.PrefetchScalarGridSpec(
            num_scalar_prefetch=1,
            grid=(tiles,),
            in_specs=specs,
            out_specs=pl.BlockSpec((rows, tile), here if partial else column),
            scratch_shapes=[pltpu.VMEM((rows, tile), F32)],
        ),
        input_output_aliases=aliases,
        compiler_params=pltpu.CompilerParams(vmem_limit_bytes=VMEM_LIMIT),
        cost_estimate=pl.CostEstimate(
            flops=2 * rows * part * depth * (len(pieces) + 1),
            bytes_accessed=2 * (part * (depth * (len(pieces) + 1) + rows)),
            transcendentals=0,
        ),
        name="product",
    )(scalars, *operands)


def payload_kernel(scalars, down_ref, up_ref, out_ref):
    part = down_ref.shape[2]
    for k in range(out_ref.shape[0] // down_ref.shape[0]):
        span = slice(k * down_ref.shape[0], (k + 1) * down_ref.shape[0])
        out_ref[span, :, :part] = down_ref[...]
        out_ref[span, :, part:] = up_ref[...]


def payload(group, down, up, n):
    owned, rank, width = down.shape
    slab, part = up.shape[2], width // 2
    return pl.pallas_call(
        payload_kernel,
        out_shape=jax.ShapeDtypeStruct((n * owned, rank, part + slab), BF16),
        grid_spec=pltpu.PrefetchScalarGridSpec(
            num_scalar_prefetch=1,
            grid=(1,),
            in_specs=[
                pl.BlockSpec((owned, rank, part), lambda i, s: (0, 0, s[0])),
                pl.BlockSpec((owned, rank, slab), lambda i, s: (0, 0, 0)),
            ],
            out_specs=pl.BlockSpec((n * owned, rank, part + slab), lambda i, s: (0, 0, 0)),
        ),
        compiler_params=pltpu.CompilerParams(vmem_limit_bytes=VMEM_LIMIT),
        name="payload",
    )(group[None], down, up)


def project(group, slab_index, slots, x, weighted, received, other):
    rows, width = x.shape
    tenants, rank, part = other.shape
    slab = received.shape[2] - part
    blocks = slots.shape[0]
    return pl.pallas_call(
        functools.partial(project_kernel, blocks),
        out_shape=jax.ShapeDtypeStruct((rows, 2 * rank), BF16),
        grid_spec=pltpu.PrefetchScalarGridSpec(
            num_scalar_prefetch=1,
            grid=(1,),
            in_specs=[
                pl.BlockSpec((rows, width), lambda i, s: (0, 0)),
                pl.BlockSpec((rows, slab), lambda i, s: (0, s[blocks + 1])),
                pl.BlockSpec((tenants, rank, part), lambda i, s: (0, 0, 0)),
                pl.BlockSpec((tenants, rank, part), lambda i, s: (0, 0, 0)),
                pl.BlockSpec((tenants, rank, slab), lambda i, s: (0, 0, part // slab)),
            ],
            out_specs=pl.BlockSpec((rows, 2 * rank), lambda i, s: (0, 0)),
        ),
        compiler_params=pltpu.CompilerParams(vmem_limit_bytes=VMEM_LIMIT),
        cost_estimate=pl.CostEstimate(
            flops=2 * rows * rank * (width + slab),
            bytes_accessed=2 * (rows + tenants * rank) * (width + slab),
            transcendentals=0,
        ),
        name="project",
    )(jnp.stack([*slots, group, slab_index]), x, weighted, received, other, received)


def adapter_grads(slab_index, slots, x, weighted, here, there, tenants, slab):
    rows, width = x.shape
    rank = here.shape[1] // 2
    blocks = slots.shape[0]
    return pl.pallas_call(
        functools.partial(grads_kernel, blocks),
        out_shape=(
            jax.ShapeDtypeStruct((tenants, rank, width + slab), BF16),
            jax.ShapeDtypeStruct((rows, rank), BF16),
        ),
        grid_spec=pltpu.PrefetchScalarGridSpec(
            num_scalar_prefetch=1,
            grid=(1,),
            in_specs=[
                pl.BlockSpec((rows, width), lambda i, s: (0, 0)),
                pl.BlockSpec((rows, slab), lambda i, s: (0, s[blocks])),
                pl.BlockSpec((rows, 2 * rank), lambda i, s: (0, 0)),
                pl.BlockSpec((rows, 2 * rank), lambda i, s: (0, 0)),
            ],
            out_specs=[
                pl.BlockSpec((tenants, rank, width + slab), lambda i, s: (0, 0, 0)),
                pl.BlockSpec((rows, rank), lambda i, s: (0, 0)),
            ],
            scratch_shapes=[pltpu.VMEM((tenants, rank, width + slab), F32)],
        ),
        compiler_params=pltpu.CompilerParams(vmem_limit_bytes=VMEM_LIMIT),
        cost_estimate=pl.CostEstimate(
            flops=2 * rows * rank * (width + slab),
            bytes_accessed=2 * (rows + tenants * rank) * (width + slab),
            transcendentals=0,
        ),
        name="adapter_grads",
    )(jnp.stack([*slots, slab_index]), x, weighted, here, there)


def sum_kernel(got_ref, down_ref, up_ref):
    width = down_ref.shape[2]
    total = got_ref[0].astype(F32)
    for k in range(1, got_ref.shape[0]):
        total += got_ref[k].astype(F32)
    down_ref[0] = total[:, :width]
    up_ref[0] = total[:, width:]


def owner_sums(got, width):
    _, rank, both = got.shape
    return pl.pallas_call(
        sum_kernel,
        out_shape=(
            jax.ShapeDtypeStruct((1, rank, width), F32),
            jax.ShapeDtypeStruct((1, rank, both - width), F32),
        ),
        compiler_params=pltpu.CompilerParams(vmem_limit_bytes=VMEM_LIMIT),
        cost_estimate=pl.CostEstimate(
            flops=got.size, bytes_accessed=2 * got.size, transcendentals=0
        ),
        name="owner_sums",
    )(got)


def gather_line(piece, n, groups):
    me = lax.axis_index("seq").astype(jnp.int32)
    mine, other, owner = [], [], []
    up = down = piece

    def keep(value, pairs, source):
        targets = [b for _, b in pairs]
        swaps = [
            (g * n + t, (groups - 1 - g) * n + t) for g in range(groups) for t in targets
        ]
        mine.append(value)
        with jax.named_scope("swap_w"):
            other.append(lax.ppermute(value, ("groups", "seq"), swaps))
        low, high = min(targets), max(targets)
        has = (me >= low) & (me <= high)
        if len(targets) < high - low + 1:
            gap = [t for t in range(low, high) if t not in targets]
            has = has & ((me < gap[0]) | (me > gap[-1]))
        owner.append(jnp.where(has, source, -1))

    for k in range(1, n):
        up_pairs = [(i, i + 1) for i in range(k - 1, n - 1)]
        down_pairs = [(i + 1, i) for i in range(n - k)]
        if {a for a, _ in up_pairs} & {a for a, _ in down_pairs}:
            with jax.named_scope(f"line_{k}"):
                up = lax.ppermute(up, "seq", up_pairs)
                down = lax.ppermute(down, "seq", down_pairs)
            keep(up, up_pairs, me - k)
            keep(down, down_pairs, me + k)
        else:
            both = jnp.where(me >= k - 1, up, down)
            with jax.named_scope(f"line_{k}"):
                up = down = lax.ppermute(both, "seq", up_pairs + down_pairs)
            keep(up, up_pairs + down_pairs, jnp.where(me >= k, me - k, me + k))
    return mine, other, owner


def per_device(
    sizes,
    layer_input,
    out_grad,
    value_weight,
    adapter_down,
    adapter_up,
    block_tenant,
    tenant_slot,
    forget_flag,
):
    n, groups = sizes
    token_rows, width = layer_input.shape
    rank = adapter_down.shape[1]
    slab = adapter_up.shape[2]
    tenants = tenant_slot.shape[0]
    depth = value_weight.shape[0]
    swap = lambda axis: functools.partial(lax.ppermute, axis_name=axis, perm=[(0, 1), (1, 0)])

    half = width // 2
    group = lax.axis_index("groups").astype(jnp.int32)
    received = lax.all_to_all(
        payload(group, adapter_down, adapter_up, n), "seq", split_axis=0, concat_axis=0, tiled=True
    )
    with jax.named_scope("swap_a"):
        swapped = swap("groups")(received[:, :, :half])

    piece = lax.dynamic_slice_in_dim(value_weight, group * half, half, 1)
    mine, other, owners = gather_line(piece, n, groups)

    row_sign = (1 - 2 * forget_flag).astype(BF16)
    weighted = out_grad * row_sign[:, None]
    tenant_ids = jnp.arange(tenants, dtype=jnp.int32)
    slots = jnp.sum(
        jnp.where(block_tenant == tenant_ids[None, :], tenant_slot[None, :], 0), axis=1
    ).astype(jnp.int32)
    slab_index = lax.axis_index(("tensor", "pipe")).astype(jnp.int32)
    me = lax.axis_index("seq").astype(jnp.int32)

    part = project(group, slab_index, slots, layer_input, weighted, received, swapped)
    here = part
    axes = [a for a in ("pipe", "tensor")]
    for axis in axes[:-1]:
        here = (here.astype(F32) + line_sum_rest(here, axis, sizes)).astype(BF16)
    there = line_sum_rest(here, axes[-1], sizes).astype(BF16)
    there, _ = lax.optimization_barrier((there, (mine[:4], other[:1])))
    table, low_b = adapter_grads(
        slab_index, slots, layer_input, weighted, here, there, tenants, slab
    )
    got = lax.all_to_all(table, "seq", split_axis=0, concat_axis=0, tiled=True)
    down_grad, up_grad = owner_sums(got, width)

    opening = lambda down: (low_b, down, value_weight)
    first = product(group, slots, me, owners, weighted, mine, opening(received), width)
    rest = product(
        1 - group,
        slots,
        me,
        owners[:-1],
        weighted,
        other[:-1],
        opening(swapped),
        width,
        partial=True,
    )
    full = product(1 - group, slots, me, owners[-1:], weighted, other[-1:], rest, width, first)
    return full, down_grad, up_grad


def line_sum_rest(value, axis, sizes):
    size = lax.axis_size(axis)
    rest = 0.0
    for d in range(1, size):
        rest = rest + lax.ppermute(
            value, axis, [(i, (i + d) % size) for i in range(size)]
        ).astype(F32)
    return rest


def solution(mesh):
    sizes = (mesh.shape["seq"], mesh.shape["groups"])
    return jax.shard_map(
        functools.partial(per_device, sizes),
        mesh=mesh,
        in_specs=(
            P(("groups", "seq"), ("tensor", "pipe")),
            P(("groups", "seq"), None),
            P("seq", ("tensor", "pipe")),
            P("seq", None, ("tensor", "pipe")),
            P("seq", None, ("tensor", "pipe")),
            P(("groups", "seq"), None),
            P(),
            P(("groups", "seq")),
        ),
        out_specs=(
            P(("groups", "seq"), ("tensor", "pipe")),
            P(("groups", "seq"), None, ("tensor", "pipe")),
            P(("groups", "seq"), None, ("tensor", "pipe")),
        ),
        check_vma=False,
    )
```

```python
import functools

import jax
import jax.numpy as jnp
from jax import lax
from jax.experimental import pallas as pl
from jax.experimental.pallas import tpu as pltpu
from jax.sharding import PartitionSpec as P

SCALE = 2.0
VMEM_LIMIT = 48 << 20
F32 = jnp.float32
BF16 = jnp.bfloat16


ROWS_BY_ROWS = (((1,), (1,)), ((), ()))
COLUMNS_BY_COLUMNS = (((0,), (0,)), ((), ()))


def low_kernel(blocks, scalars, w_ref, up_ref, out_ref):
    rows = w_ref.shape[0] // blocks
    for b in range(blocks):
        span = slice(b * rows, (b + 1) * rows)
        out_ref[span, :] = lax.dot_general(
            w_ref[span, :], up_ref[scalars[b]], ROWS_BY_ROWS, preferred_element_type=F32
        ).astype(BF16)


def hidden_kernel(blocks, scalars, x_ref, mine_ref, other_ref, out_ref):
    rows = x_ref.shape[0] // blocks
    part = mine_ref.shape[2]

    def run(first, second):
        for b in range(blocks):
            s = scalars[b]
            span = slice(b * rows, (b + 1) * rows)
            hidden = lax.dot_general(
                x_ref[span, :part], first[s], ROWS_BY_ROWS, preferred_element_type=F32
            ) + lax.dot_general(
                x_ref[span, part:], second[s], ROWS_BY_ROWS, preferred_element_type=F32
            )
            out_ref[span, :] = hidden.astype(BF16)

    @pl.when(scalars[blocks] == 0)
    def _():
        run(mine_ref, other_ref)

    @pl.when(scalars[blocks] != 0)
    def _():
        run(other_ref, mine_ref)


def grads_kernel(blocks, scale_rank, scalars, x_ref, here_ref, there_ref, table_ref, *rest):
    acc_ref = rest[-1]
    rows = x_ref.shape[0] // blocks
    total = here_ref[...].astype(F32) + there_ref[...].astype(F32)
    ranks = (SCALE * total if scale_rank else total).astype(BF16)
    if scale_rank:
        rest[0][...] = ranks
    acc_ref[...] = jnp.zeros_like(acc_ref)
    for b in range(blocks):
        span = slice(b * rows, (b + 1) * rows)
        acc_ref[scalars[b]] += lax.dot_general(
            ranks[span], x_ref[span, :], COLUMNS_BY_COLUMNS, preferred_element_type=F32
        )
    table = acc_ref[...] if scale_rank else SCALE * acc_ref[...]
    table_ref[...] = table.astype(BF16)


def product_kernel(plan, scalars, *refs):
    count, blocks, opens, aligned = plan
    refs = list(refs)
    weighted_ref = refs.pop(0)
    acc_ref, out_ref = refs.pop(), refs.pop()
    if opens:
        low_ref, down_ref, own_ref = refs[:3]
        pieces = refs[3 : 3 + count]
        depth = own_ref.shape[0]
        block_rows = low_ref.shape[0] // blocks
        own = take_columns(weighted_ref, scalars[blocks + 1], 0, depth, aligned)
        acc_ref[...] = jnp.dot(own, own_ref[...], preferred_element_type=F32)
        for b in range(blocks):
            span = slice(b * block_rows, (b + 1) * block_rows)
            acc_ref[span, :] += jnp.dot(
                low_ref[span, :], down_ref[scalars[b]], preferred_element_type=F32
            )
    else:
        pieces = refs[1 : 1 + count]
        depth = pieces[0].shape[0]
        acc_ref[...] = refs[0][...]
    for j, piece in enumerate(pieces):
        owner = scalars[blocks + 2 + j]

        @pl.when(owner >= 0)
        def _(j=j, piece=piece, owner=owner):
            columns = take_columns(weighted_ref, owner, j + 1, depth, aligned)
            acc_ref[...] += jnp.dot(columns, piece[...], preferred_element_type=F32)

    out_ref[...] = acc_ref[...].astype(out_ref.dtype)


def take_columns(ref, owner, position, depth, aligned):
    if aligned:
        return ref[:, pl.ds(pl.multiple_of(owner * depth, 128), depth)]
    return ref[:, position * depth : (position + 1) * depth]


def product(half, slots, me, owners, weighted, pieces, start, width, into=None, partial=False):
    opens = isinstance(start, tuple)
    rows = weighted.shape[0]
    depth = pieces[0].shape[0]
    part = width // 2
    tile = min(512, part)
    tiles = part // tile
    blocks = slots.shape[0]
    aligned = depth % 128 == 0
    if not aligned:
        begins = [me] + [jnp.maximum(o, 0) for o in owners]
        weighted = jnp.concatenate(
            [lax.dynamic_slice_in_dim(weighted, o * depth, depth, 1) for o in begins], axis=1
        )
    scalars = jnp.stack([*slots, half, me, *owners])
    whole = lambda i, s: (0, 0)
    here = lambda i, s: (0, i)
    column = lambda i, s: (0, s[blocks] * tiles + i)
    specs = [pl.BlockSpec(weighted.shape, whole)]
    operands = [weighted]
    if opens:
        low_b, down, own = start
        specs += [
            pl.BlockSpec(low_b.shape, whole),
            pl.BlockSpec((*down.shape[:2], tile), lambda i, s: (0, 0, i)),
            pl.BlockSpec((depth, tile), column),
        ]
        operands += [low_b, down, own]
    else:
        specs.append(pl.BlockSpec((rows, tile), here))
        operands.append(start)
    specs += [pl.BlockSpec((depth, tile), here) for _ in pieces]
    operands += pieces
    aliases = {}
    if into is not None:
        specs.append(pl.BlockSpec(memory_space=pl.ANY))
        operands.append(into)
        aliases = {len(operands): 0}
    shape = jax.ShapeDtypeStruct((rows, part), F32) if partial else jax.ShapeDtypeStruct((rows, width), BF16)
    return pl.pallas_call(
        functools.partial(product_kernel, (len(pieces), blocks, opens, aligned)),
        out_shape=shape,
        grid_spec=pltpu.PrefetchScalarGridSpec(
            num_scalar_prefetch=1,
            grid=(tiles,),
            in_specs=specs,
            out_specs=pl.BlockSpec((rows, tile), here if partial else column),
            scratch_shapes=[pltpu.VMEM((rows, tile), F32)],
        ),
        input_output_aliases=aliases,
        compiler_params=pltpu.CompilerParams(vmem_limit_bytes=VMEM_LIMIT),
        cost_estimate=pl.CostEstimate(
            flops=2 * rows * part * depth * (len(pieces) + 1),
            bytes_accessed=2 * (part * (depth * (len(pieces) + 1) + rows)),
            transcendentals=0,
        ),
        name="product",
    )(scalars, *operands)


def call(kernel, name, out_shape, scalars, operands, specs=None, scratch=(), flops=0, moved=0):
    whole = lambda shape: pl.BlockSpec(shape, lambda i, s: (0,) * len(shape))
    specs = specs or [whole(o.shape) for o in operands]
    single = isinstance(out_shape, jax.ShapeDtypeStruct)
    return pl.pallas_call(
        kernel,
        out_shape=out_shape,
        grid_spec=pltpu.PrefetchScalarGridSpec(
            num_scalar_prefetch=1,
            grid=(1,),
            in_specs=specs,
            out_specs=whole(out_shape.shape) if single else [whole(o.shape) for o in out_shape],
            scratch_shapes=list(scratch),
        ),
        compiler_params=pltpu.CompilerParams(vmem_limit_bytes=VMEM_LIMIT),
        cost_estimate=pl.CostEstimate(flops=flops, bytes_accessed=moved, transcendentals=0),
        name=name,
    )(scalars, *operands)


def bf16(*shape):
    return jax.ShapeDtypeStruct(shape, BF16)


def low_partial(slab_index, slots, weighted, up):
    rows, (_, rank, slab) = weighted.shape[0], up.shape
    blocks = slots.shape[0]
    specs = [
        pl.BlockSpec((rows, slab), lambda i, s: (0, s[blocks])),
        pl.BlockSpec(up.shape, lambda i, s: (0, 0, 0)),
    ]
    return call(
        functools.partial(low_kernel, blocks),
        "low_partial",
        bf16(rows, rank),
        jnp.stack([*slots, slab_index]),
        [weighted, up],
        specs,
        flops=2 * rows * rank * slab,
        moved=2 * (rows * slab + up.size),
    )


def hidden_partial(group, slots, x, mine, other):
    rows, width = x.shape
    rank = mine.shape[1]
    return call(
        functools.partial(hidden_kernel, slots.shape[0]),
        "hidden_partial",
        bf16(rows, rank),
        jnp.stack([*slots, group]),
        [x, mine, other],
        flops=2 * rows * rank * width,
        moved=2 * (x.size + 2 * mine.size),
    )


def down_table(slots, x, here, there, tenants):
    rows, width = x.shape
    rank = here.shape[1]
    return call(
        functools.partial(grads_kernel, slots.shape[0], True),
        "down_table",
        (bf16(tenants, rank, width), bf16(rows, rank)),
        slots,
        [x, here, there],
        scratch=[pltpu.VMEM((tenants, rank, width), F32)],
        flops=2 * rows * rank * width,
        moved=2 * (x.size + tenants * rank * width),
    )


def up_table(slab_index, slots, weighted, here, there, tenants, slab):
    rows, rank = here.shape
    blocks = slots.shape[0]
    specs = [pl.BlockSpec((rows, slab), lambda i, s: (0, s[blocks]))]
    specs += [pl.BlockSpec((rows, rank), lambda i, s: (0, 0))] * 2
    return call(
        functools.partial(grads_kernel, blocks, False),
        "up_table",
        bf16(tenants, rank, slab),
        jnp.stack([*slots, slab_index]),
        [weighted, here, there],
        specs,
        scratch=[pltpu.VMEM((tenants, rank, slab), F32)],
        flops=2 * rows * rank * slab,
        moved=2 * (rows * slab + tenants * rank * slab),
    )


def owner_sum(got, n):
    owned = got.shape[0] // n
    return jnp.sum(got.astype(F32).reshape(n, owned, *got.shape[1:]), axis=0)


def everyone(value, n):
    copies = jnp.broadcast_to(value, (n,) + value.shape).reshape(-1, *value.shape[1:])
    return lax.all_to_all(copies, "seq", split_axis=0, concat_axis=0, tiled=True)


def edge_pairs(parity, k, n):
    pairs = []
    for i in range(parity, n - 1, 2):
        if i >= k - 1:
            pairs.append((i, i + 1))
        if i + 1 <= n - k:
            pairs.append((i + 1, i))
    return pairs


def swap_pairs(pairs, n, groups):
    targets = [b for _, b in pairs]
    return [(g * n + t, (groups - 1 - g) * n + t) for g in range(groups) for t in targets]


def after(value, *others):
    return lax.optimization_barrier((value, others))[0]


def psum_halves(value):
    here = (value.astype(F32) + rest_of(value, "pipe")).astype(BF16)
    return here, rest_of(here, "tensor").astype(BF16)


def rest_of(value, axis):
    size = lax.axis_size(axis)
    rest = 0.0
    for d in range(1, size):
        pairs = [(i, (i + d) % size) for i in range(size)]
        with jax.named_scope(f"psum_{axis}"):
            rest = rest + lax.ppermute(value, axis, pairs).astype(F32)
    return rest


def per_device(
    sizes,
    layer_input,
    out_grad,
    value_weight,
    adapter_down,
    adapter_up,
    block_tenant,
    tenant_slot,
    forget_flag,
):
    n, groups = sizes
    token_rows, width = layer_input.shape
    rank = adapter_down.shape[1]
    slab = adapter_up.shape[2]
    tenants = tenant_slot.shape[0]
    depth = value_weight.shape[0]
    swap = lambda axis: functools.partial(lax.ppermute, axis_name=axis, perm=[(0, 1), (1, 0)])

    half = width // 2
    group = lax.axis_index("groups").astype(jnp.int32)
    me = lax.axis_index("seq").astype(jnp.int32)
    slab_index = lax.axis_index(("tensor", "pipe")).astype(jnp.int32)
    columns = lambda a: lax.dynamic_slice_in_dim(a, group * half, half, a.ndim - 1)

    with jax.named_scope("all_up"):
        up = everyone(adapter_up, n)
    row_sign = (1 - 2 * forget_flag).astype(BF16)
    weighted = out_grad * row_sign[:, None]
    tenant_ids = jnp.arange(tenants, dtype=jnp.int32)
    slots = jnp.sum(
        jnp.where(block_tenant == tenant_ids[None, :], tenant_slot[None, :], 0), axis=1
    ).astype(jnp.int32)

    arrived, owners, pairs_of = [], [], []
    last = [columns(value_weight)] * 2
    for k in range(1, n):
        new = [None, None]
        for parity in (0, 1):
            pairs = edge_pairs(parity, k, n)
            if not pairs:
                continue
            with jax.named_scope(f"line_{k}_{parity}"):
                new[parity] = lax.ppermute(last[1 - parity], "seq", pairs)
            from_left = me % 2 != parity
            owner = jnp.where(from_left, me - k, me + k)
            arrived.append(new[parity])
            pairs_of.append(pairs)
            owners.append(jnp.where((owner >= 0) & (owner < n), owner, -1))
        last = new
    swapped = []
    for value, pairs in zip(arrived, pairs_of):
        with jax.named_scope("swap_w"):
            swapped.append(lax.ppermute(value, ("groups", "seq"), swap_pairs(pairs, n, groups)))

    with jax.named_scope("all_down"):
        own_half = after(columns(adapter_down), up)
        down_mine = everyone(own_half, n)

    with jax.named_scope("low"):
        here, there = psum_halves(low_partial(slab_index, slots, weighted, up))
        there = after(there, arrived[:2], down_mine)
        table, low_b = down_table(slots, layer_input, here, there, tenants)
        got_down = lax.all_to_all(table, "seq", split_axis=0, concat_axis=0, tiled=True)

    with jax.named_scope("swap_a"):
        down_other = swap("groups")(down_mine)
        down_other = after(down_other, arrived[2:4], swapped[0])
    with jax.named_scope("hidden"):
        here, there = psum_halves(
            hidden_partial(group, slots, layer_input, down_mine, down_other)
        )
        there = after(there, got_down, arrived[4:5], swapped[1:2])
        table = up_table(slab_index, slots, weighted, here, there, tenants, slab)
        got_up = lax.all_to_all(table, "seq", split_axis=0, concat_axis=0, tiled=True)

    opening = lambda down: (low_b, down, value_weight)
    first = product(group, slots, me, owners, weighted, arrived, opening(down_mine), width)
    rest = product(
        1 - group,
        slots,
        me,
        owners[:-1],
        weighted,
        swapped[:-1],
        opening(down_other),
        width,
        partial=True,
    )
    full = product(1 - group, slots, me, owners[-1:], weighted, swapped[-1:], rest, width, first)
    return full, owner_sum(got_down, n), owner_sum(got_up, n)


def solution(mesh):
    sizes = (mesh.shape["seq"], mesh.shape["groups"])
    return jax.shard_map(
        functools.partial(per_device, sizes),
        mesh=mesh,
        in_specs=(
            P(("groups", "seq"), ("tensor", "pipe")),
            P(("groups", "seq"), None),
            P("seq", ("tensor", "pipe")),
            P("seq", None, ("tensor", "pipe")),
            P("seq", None, ("tensor", "pipe")),
            P(("groups", "seq"), None),
            P(),
            P(("groups", "seq")),
        ),
        out_specs=(
            P(("groups", "seq"), ("tensor", "pipe")),
            P(("groups", "seq"), None, ("tensor", "pipe")),
            P(("groups", "seq"), None, ("tensor", "pipe")),
        ),
        check_vma=False,
    )
```

```python
import functools

import jax
import jax.numpy as jnp
from jax import lax
from jax.experimental import pallas as pl
from jax.experimental.pallas import tpu as pltpu
from jax.sharding import PartitionSpec as P

SCALE = 2.0
VMEM_LIMIT = 48 << 20
F32 = jnp.float32
BF16 = jnp.bfloat16


ROWS_BY_ROWS = (((1,), (1,)), ((), ()))
COLUMNS_BY_COLUMNS = (((0,), (0,)), ((), ()))


def payload_kernel(scalars, down_ref, up_ref, out_ref):
    owned, _, part = down_ref.shape
    for k in range(out_ref.shape[0] // owned):
        span = slice(k * owned, (k + 1) * owned)
        out_ref[span, :, :part] = down_ref[...]
        out_ref[span, :, part:] = up_ref[...]


def project_kernel(blocks, scalars, x_ref, w_ref, mine_ref, other_ref, up_ref, out_ref):
    rows = x_ref.shape[0] // blocks
    rank, part = mine_ref.shape[1:]

    def run(first, second):
        for b in range(blocks):
            s = scalars[b]
            span = slice(b * rows, (b + 1) * rows)
            hidden = lax.dot_general(
                x_ref[span, :part], first[s], ROWS_BY_ROWS, preferred_element_type=F32
            ) + lax.dot_general(
                x_ref[span, part:], second[s], ROWS_BY_ROWS, preferred_element_type=F32
            )
            low = lax.dot_general(
                w_ref[span, :], up_ref[s], ROWS_BY_ROWS, preferred_element_type=F32
            )
            out_ref[span, :rank] = hidden.astype(BF16)
            out_ref[span, rank:] = low.astype(BF16)

    @pl.when(scalars[blocks] == 0)
    def _():
        run(mine_ref, other_ref)

    @pl.when(scalars[blocks] != 0)
    def _():
        run(other_ref, mine_ref)


def grads_kernel(blocks, scalars, x_ref, w_ref, here_ref, there_ref, table_ref, low_ref, acc_ref):
    rows, width = x_ref.shape[0] // blocks, x_ref.shape[1]
    rank = low_ref.shape[1]
    total = here_ref[...].astype(F32) + there_ref[...].astype(F32)
    hidden_b = total[:, :rank].astype(BF16)
    low_b = (SCALE * total[:, rank:]).astype(BF16)
    low_ref[...] = low_b
    acc_ref[...] = jnp.zeros_like(acc_ref)
    for b in range(blocks):
        s = scalars[b]
        span = slice(b * rows, (b + 1) * rows)
        acc_ref[s, :, :width] += lax.dot_general(
            low_b[span], x_ref[span, :], COLUMNS_BY_COLUMNS, preferred_element_type=F32
        )
        acc_ref[s, :, width:] += SCALE * lax.dot_general(
            hidden_b[span], w_ref[span, :], COLUMNS_BY_COLUMNS, preferred_element_type=F32
        )
    table_ref[...] = acc_ref[...].astype(BF16)


def sum_kernel(got_ref, down_ref, up_ref):
    count = got_ref.shape[0] // down_ref.shape[0]
    owned, _, width = down_ref.shape
    total = got_ref[:owned].astype(F32)
    for k in range(1, count):
        total += got_ref[k * owned : (k + 1) * owned].astype(F32)
    down_ref[...] = total[:, :, :width]
    up_ref[...] = total[:, :, width:]


def product_kernel(
    blocks, tiles, scalars, weighted_ref, low_ref, down_ref, own_ref, *refs
):
    out_ref, whole_ref, sems = refs[-3:]
    part = whole_ref.shape[1]
    tile = part // tiles
    pieces = refs[: scalars.shape[0] - blocks - 2]
    half = scalars[blocks]
    rows = weighted_ref.shape[0] // blocks

    def each(t, act):
        columns = pl.ds(t * tile, tile)
        own_columns = pl.ds(pl.multiple_of(half * part + t * tile, 128), tile)
        for j, source in enumerate([own_ref.at[:, own_columns]] + [p.at[:, columns] for p in pieces]):
            begin = scalars[blocks + 1 + j]

            def run(j=j, source=source, begin=begin):
                place = pl.ds(pl.multiple_of(begin, 16), source.shape[0])
                copy = pltpu.make_async_copy(source, whole_ref.at[place, columns], sems.at[t, j])
                copy.start() if act == "start" else copy.wait()

            if j:
                pl.when(begin >= 0)(run)
            else:
                run()

    for t in range(tiles):
        each(t, "start")
    for t in range(tiles):
        each(t, "wait")
        columns = slice(t * tile, (t + 1) * tile)
        total = jnp.dot(weighted_ref[...], whole_ref[:, columns], preferred_element_type=F32)
        for b in range(blocks):
            span = slice(b * rows, (b + 1) * rows)
            term = jnp.dot(
                low_ref[span, :], down_ref[scalars[b], :, columns], preferred_element_type=F32
            )
            out_ref[span, columns] = (total[span] + term).astype(BF16)


def product(half, slots, begins, weighted, low_b, down, own, pieces, into=None):
    rows = weighted.shape[0]
    width = own.shape[1]
    part = width // 2
    tiles = 2 if part % 256 == 0 else 1
    blocks = slots.shape[0]
    whole = lambda i, s: (0, 0)
    specs = [
        pl.BlockSpec(weighted.shape, whole),
        pl.BlockSpec(low_b.shape, whole),
        pl.BlockSpec((*down.shape[:2], part), lambda i, s: (0, 0, 0)),
    ] + [pl.BlockSpec(memory_space=pl.ANY) for _ in [own, *pieces]]
    operands = [weighted, low_b, down, own, *pieces]
    aliases = {}
    if into is not None:
        specs.append(pl.BlockSpec(memory_space=pl.ANY))
        operands.append(into)
        aliases = {len(operands): 0}
    return pl.pallas_call(
        functools.partial(product_kernel, blocks, tiles),
        out_shape=bf16(rows, width),
        grid_spec=pltpu.PrefetchScalarGridSpec(
            num_scalar_prefetch=1,
            grid=(1,),
            in_specs=specs,
            out_specs=pl.BlockSpec((rows, part), lambda i, s: (0, s[blocks])),
            scratch_shapes=[
                pltpu.VMEM((weighted.shape[1], part), BF16),
                pltpu.SemaphoreType.DMA((tiles, len(pieces) + 1)),
            ],
        ),
        input_output_aliases=aliases,
        compiler_params=pltpu.CompilerParams(vmem_limit_bytes=VMEM_LIMIT),
        cost_estimate=pl.CostEstimate(
            flops=24 * rows * part * weighted.shape[1],
            bytes_accessed=2 * part * (weighted.shape[1] + rows),
            transcendentals=0,
        ),
        name="product",
    )(jnp.stack([*slots, half, *begins]), *operands)


def call(kernel, name, out_shape, scalars, operands, specs=None, scratch=(), flops=0, moved=0):
    whole = lambda shape: pl.BlockSpec(shape, lambda i, s: (0,) * len(shape))
    specs = specs or [whole(o.shape) for o in operands]
    single = isinstance(out_shape, jax.ShapeDtypeStruct)
    return pl.pallas_call(
        kernel,
        out_shape=out_shape,
        grid_spec=pltpu.PrefetchScalarGridSpec(
            num_scalar_prefetch=1,
            grid=(1,),
            in_specs=specs,
            out_specs=whole(out_shape.shape) if single else [whole(o.shape) for o in out_shape],
            scratch_shapes=list(scratch),
        ),
        compiler_params=pltpu.CompilerParams(vmem_limit_bytes=VMEM_LIMIT),
        cost_estimate=pl.CostEstimate(flops=flops, bytes_accessed=moved, transcendentals=0),
        name=name,
    )(scalars, *operands)


def bf16(*shape):
    return jax.ShapeDtypeStruct(shape, BF16)


def payload(group, down, up, n):
    owned, rank, width = down.shape
    slab, part = up.shape[2], width // 2
    specs = [
        pl.BlockSpec((owned, rank, part), lambda i, s: (0, 0, s[0])),
        pl.BlockSpec((owned, rank, slab), lambda i, s: (0, 0, 0)),
    ]
    shape = bf16(n * owned, rank, part + slab)
    return call(payload_kernel, "payload", shape, group[None], [down, up], specs)


def project(group, slab_index, slots, x, weighted, received, other):
    rows, width = x.shape
    tenants, rank, part = other.shape
    slab = received.shape[2] - part
    blocks = slots.shape[0]
    whole = lambda i, s: (0, 0, 0)
    specs = [
        pl.BlockSpec((rows, width), lambda i, s: (0, 0)),
        pl.BlockSpec((rows, slab), lambda i, s: (0, s[blocks + 1])),
        pl.BlockSpec((tenants, rank, part), whole),
        pl.BlockSpec((tenants, rank, part), whole),
        pl.BlockSpec((tenants, rank, slab), lambda i, s: (0, 0, part // slab)),
    ]
    return call(
        functools.partial(project_kernel, blocks),
        "project",
        bf16(rows, 2 * rank),
        jnp.stack([*slots, group, slab_index]),
        [x, weighted, received, other, received],
        specs,
        flops=2 * rows * rank * (width + slab),
        moved=2 * (rows + tenants * rank) * (width + slab),
    )


def adapter_grads(slab_index, slots, x, weighted, here, there, tenants, slab):
    rows, width = x.shape
    rank = here.shape[1] // 2
    blocks = slots.shape[0]
    ranks = pl.BlockSpec((rows, 2 * rank), lambda i, s: (0, 0))
    specs = [
        pl.BlockSpec((rows, width), lambda i, s: (0, 0)),
        pl.BlockSpec((rows, slab), lambda i, s: (0, s[blocks])),
        ranks,
        ranks,
    ]
    return call(
        functools.partial(grads_kernel, blocks),
        "adapter_grads",
        (bf16(tenants, rank, width + slab), bf16(rows, rank)),
        jnp.stack([*slots, slab_index]),
        [x, weighted, here, there],
        specs,
        scratch=[pltpu.VMEM((tenants, rank, width + slab), F32)],
        flops=2 * rows * rank * (width + slab),
        moved=2 * (rows + tenants * rank) * (width + slab),
    )


def owner_sums(got, n, width):
    tenants, rank, both = got.shape
    owned = tenants // n
    return pl.pallas_call(
        sum_kernel,
        out_shape=(
            jax.ShapeDtypeStruct((owned, rank, width), F32),
            jax.ShapeDtypeStruct((owned, rank, both - width), F32),
        ),
        compiler_params=pltpu.CompilerParams(vmem_limit_bytes=VMEM_LIMIT),
        cost_estimate=pl.CostEstimate(
            flops=got.size, bytes_accessed=2 * got.size, transcendentals=0
        ),
        name="owner_sums",
    )(got)


def edge_pairs(parity, k, n):
    pairs = []
    for i in range(parity, n - 1, 2):
        if i >= k - 1:
            pairs.append((i, i + 1))
        if i + 1 <= n - k:
            pairs.append((i + 1, i))
    return pairs


def swap_pairs(pairs, n, groups):
    targets = [b for _, b in pairs]
    return [(g * n + t, (groups - 1 - g) * n + t) for g in range(groups) for t in targets]


def after(value, *others):
    return lax.optimization_barrier((value, others))[0]


def pair_sum(value):
    return (value.astype(F32) + rest_of(value, "pipe")).astype(BF16)


def rest_of(value, axis):
    size = lax.axis_size(axis)
    rest = 0.0
    for d in range(1, size):
        pairs = [(i, (i + d) % size) for i in range(size)]
        with jax.named_scope(f"psum_{axis}"):
            rest = rest + lax.ppermute(value, axis, pairs).astype(F32)
    return rest


def per_device(
    sizes,
    layer_input,
    out_grad,
    value_weight,
    adapter_down,
    adapter_up,
    block_tenant,
    tenant_slot,
    forget_flag,
):
    n, groups = sizes
    token_rows, width = layer_input.shape
    rank = adapter_down.shape[1]
    slab = adapter_up.shape[2]
    tenants = tenant_slot.shape[0]
    depth = value_weight.shape[0]
    swap = lambda axis: functools.partial(lax.ppermute, axis_name=axis, perm=[(0, 1), (1, 0)])

    half = width // 2
    group = lax.axis_index("groups").astype(jnp.int32)
    me = lax.axis_index("seq").astype(jnp.int32)
    slab_index = lax.axis_index(("tensor", "pipe")).astype(jnp.int32)
    columns = lambda a: lax.dynamic_slice_in_dim(a, group * half, half, a.ndim - 1)

    with jax.named_scope("adapters"):
        received = lax.all_to_all(
            payload(group, adapter_down, adapter_up, n),
            "seq",
            split_axis=0,
            concat_axis=0,
            tiled=True,
        )
    with jax.named_scope("swap_a"):
        down_other = swap("groups")(received[:, :, :half])

    row_sign = (1 - 2 * forget_flag).astype(BF16)
    weighted = out_grad * row_sign[:, None]
    tenant_ids = jnp.arange(tenants, dtype=jnp.int32)
    slots = jnp.sum(
        jnp.where(block_tenant == tenant_ids[None, :], tenant_slot[None, :], 0), axis=1
    ).astype(jnp.int32)

    depth = value_weight.shape[0]
    arrived, begins, pairs_of = [], [me * depth], []

    def advance(k, last, *before):
        last, new = after(last, before), [None, None]
        for parity in (0, 1):
            pairs = edge_pairs(parity, k, n)
            if not pairs:
                continue
            owner = jnp.where(me % 2 != parity, me - k, me + k)
            with jax.named_scope(f"line_{k}_{parity}"):
                new[parity] = lax.ppermute(last[1 - parity], "seq", pairs)
            arrived.append(new[parity])
            pairs_of.append(pairs)
            begins.append(jnp.where((owner >= 0) & (owner < n), owner * depth, -1))
        return new

    def exchange(j, *before):
        with jax.named_scope(f"swap_w_{j}"):
            return lax.ppermute(
                after(arrived[j], before), ("groups", "seq"), swap_pairs(pairs_of[j], n, groups)
            )

    last = advance(1, [columns(value_weight)] * 2)
    for k in range(2, n - 1):
        last = advance(k, last, received)
    with jax.named_scope("ranks"):
        part = project(group, slab_index, slots, layer_input, weighted, received, down_other)
        here = pair_sum(part)
        advance(n - 1, last, here)
        there = rest_of(here, "tensor").astype(BF16)
        table, low_b = adapter_grads(
            slab_index, slots, layer_input, weighted, here, there, tenants, slab
        )
        got = lax.all_to_all(table, "seq", split_axis=0, concat_axis=0, tiled=True)
    swapped = []
    for j in range(len(arrived)):
        before = [down_other] if j < 2 else [table] if j < 4 else []
        swapped.append(exchange(j, *before))

    common = (slots, begins, weighted, low_b)
    first = product(group, *common, received, value_weight, arrived)
    full = product(1 - group, *common, down_other, value_weight, swapped, first)
    down_grad, up_grad = owner_sums(got, n, width)
    return full, down_grad, up_grad


def solution(mesh):
    sizes = (mesh.shape["seq"], mesh.shape["groups"])
    return jax.shard_map(
        functools.partial(per_device, sizes),
        mesh=mesh,
        in_specs=(
            P(("groups", "seq"), ("tensor", "pipe")),
            P(("groups", "seq"), None),
            P("seq", ("tensor", "pipe")),
            P("seq", None, ("tensor", "pipe")),
            P("seq", None, ("tensor", "pipe")),
            P(("groups", "seq"), None),
            P(),
            P(("groups", "seq")),
        ),
        out_specs=(
            P(("groups", "seq"), ("tensor", "pipe")),
            P(("groups", "seq"), None, ("tensor", "pipe")),
            P(("groups", "seq"), None, ("tensor", "pipe")),
        ),
        check_vma=False,
    )
```

```python
import functools

import jax
import jax.numpy as jnp
from jax import lax
from jax.experimental import pallas as pl
from jax.experimental.pallas import tpu as pltpu
from jax.sharding import PartitionSpec as P

SCALE = 2.0
VMEM_LIMIT = 48 << 20
F32 = jnp.float32
BF16 = jnp.bfloat16


ROWS_BY_ROWS = (((1,), (1,)), ((), ()))
COLUMNS_BY_COLUMNS = (((0,), (0,)), ((), ()))


def payload_kernel(scalars, down_ref, up_ref, out_ref):
    owned, _, part = down_ref.shape
    for k in range(out_ref.shape[0] // owned):
        span = slice(k * owned, (k + 1) * owned)
        out_ref[span, :, :part] = down_ref[...]
        out_ref[span, :, part:] = up_ref[...]


def project_kernel(blocks, scalars, x_ref, w_ref, mine_ref, other_ref, up_ref, out_ref):
    rows = x_ref.shape[0] // blocks
    rank, part = mine_ref.shape[1:]

    def run(first, second):
        for b in range(blocks):
            s = scalars[b]
            span = slice(b * rows, (b + 1) * rows)
            hidden = lax.dot_general(
                x_ref[span, :part], first[s], ROWS_BY_ROWS, preferred_element_type=F32
            ) + lax.dot_general(
                x_ref[span, part:], second[s], ROWS_BY_ROWS, preferred_element_type=F32
            )
            low = lax.dot_general(
                w_ref[span, :], up_ref[s], ROWS_BY_ROWS, preferred_element_type=F32
            )
            out_ref[span, :rank] = hidden.astype(BF16)
            out_ref[span, rank:] = low.astype(BF16)

    @pl.when(scalars[blocks] == 0)
    def _():
        run(mine_ref, other_ref)

    @pl.when(scalars[blocks] != 0)
    def _():
        run(other_ref, mine_ref)


def grads_kernel(blocks, scalars, x_ref, w_ref, here_ref, there_ref, table_ref, low_ref, acc_ref):
    rows, width = x_ref.shape[0] // blocks, x_ref.shape[1]
    rank = low_ref.shape[1]
    total = here_ref[...].astype(F32) + there_ref[...].astype(F32)
    hidden_b = total[:, :rank].astype(BF16)
    low_b = (SCALE * total[:, rank:]).astype(BF16)
    low_ref[...] = low_b
    acc_ref[...] = jnp.zeros_like(acc_ref)
    for b in range(blocks):
        s = scalars[b]
        span = slice(b * rows, (b + 1) * rows)
        acc_ref[s, :, :width] += lax.dot_general(
            low_b[span], x_ref[span, :], COLUMNS_BY_COLUMNS, preferred_element_type=F32
        )
        acc_ref[s, :, width:] += SCALE * lax.dot_general(
            hidden_b[span], w_ref[span, :], COLUMNS_BY_COLUMNS, preferred_element_type=F32
        )
    table_ref[...] = acc_ref[...].astype(BF16)


def sum_kernel(got_ref, down_ref, up_ref):
    count = got_ref.shape[0] // down_ref.shape[0]
    owned, _, width = down_ref.shape
    total = got_ref[:owned].astype(F32)
    for k in range(1, count):
        total += got_ref[k * owned : (k + 1) * owned].astype(F32)
    down_ref[...] = total[:, :, :width]
    up_ref[...] = total[:, :, width:]


def product_kernel(
    blocks, tiles, scalars, weighted_ref, low_ref, down_ref, own_ref, *refs
):
    out_ref, whole_ref, sems = refs[-3:]
    part = whole_ref.shape[1]
    tile = part // tiles
    pieces = refs[: scalars.shape[0] - blocks - 2]
    half = scalars[blocks]
    rows = weighted_ref.shape[0] // blocks

    def each(t, act):
        columns = pl.ds(t * tile, tile)
        own_columns = pl.ds(pl.multiple_of(half * part + t * tile, 128), tile)
        for j, source in enumerate([own_ref.at[:, own_columns]] + [p.at[:, columns] for p in pieces]):
            begin = scalars[blocks + 1 + j]

            def run(j=j, source=source, begin=begin):
                place = pl.ds(pl.multiple_of(begin, 16), source.shape[0])
                copy = pltpu.make_async_copy(source, whole_ref.at[place, columns], sems.at[t, j])
                copy.start() if act == "start" else copy.wait()

            if j:
                pl.when(begin >= 0)(run)
            else:
                run()

    for t in range(tiles):
        each(t, "start")
    for t in range(tiles):
        each(t, "wait")
        columns = slice(t * tile, (t + 1) * tile)
        total = jnp.dot(weighted_ref[...], whole_ref[:, columns], preferred_element_type=F32)
        for b in range(blocks):
            span = slice(b * rows, (b + 1) * rows)
            term = jnp.dot(
                low_ref[span, :], down_ref[scalars[b], :, columns], preferred_element_type=F32
            )
            out_ref[span, columns] = (total[span] + term).astype(BF16)


def product(half, slots, begins, weighted, low_b, down, own, pieces, into=None):
    rows = weighted.shape[0]
    width = own.shape[1]
    part = width // 2
    tiles = 2 if part % 256 == 0 else 1
    blocks = slots.shape[0]
    whole = lambda i, s: (0, 0)
    specs = [
        pl.BlockSpec(weighted.shape, whole),
        pl.BlockSpec(low_b.shape, whole),
        pl.BlockSpec((*down.shape[:2], part), lambda i, s: (0, 0, 0)),
    ] + [pl.BlockSpec(memory_space=pl.ANY) for _ in [own, *pieces]]
    operands = [weighted, low_b, down, own, *pieces]
    aliases = {}
    if into is not None:
        specs.append(pl.BlockSpec(memory_space=pl.ANY))
        operands.append(into)
        aliases = {len(operands): 0}
    return pl.pallas_call(
        functools.partial(product_kernel, blocks, tiles),
        out_shape=bf16(rows, width),
        grid_spec=pltpu.PrefetchScalarGridSpec(
            num_scalar_prefetch=1,
            grid=(1,),
            in_specs=specs,
            out_specs=pl.BlockSpec((rows, part), lambda i, s: (0, s[blocks])),
            scratch_shapes=[
                pltpu.VMEM((weighted.shape[1], part), BF16),
                pltpu.SemaphoreType.DMA((tiles, len(pieces) + 1)),
            ],
        ),
        input_output_aliases=aliases,
        compiler_params=pltpu.CompilerParams(vmem_limit_bytes=VMEM_LIMIT),
        cost_estimate=pl.CostEstimate(
            flops=24 * rows * part * weighted.shape[1],
            bytes_accessed=2 * part * (weighted.shape[1] + rows),
            transcendentals=0,
        ),
        name="product",
    )(jnp.stack([*slots, half, *begins]), *operands)


def call(kernel, name, out_shape, scalars, operands, specs=None, scratch=(), flops=0, moved=0):
    whole = lambda shape: pl.BlockSpec(shape, lambda i, s: (0,) * len(shape))
    specs = specs or [whole(o.shape) for o in operands]
    single = isinstance(out_shape, jax.ShapeDtypeStruct)
    return pl.pallas_call(
        kernel,
        out_shape=out_shape,
        grid_spec=pltpu.PrefetchScalarGridSpec(
            num_scalar_prefetch=1,
            grid=(1,),
            in_specs=specs,
            out_specs=whole(out_shape.shape) if single else [whole(o.shape) for o in out_shape],
            scratch_shapes=list(scratch),
        ),
        compiler_params=pltpu.CompilerParams(vmem_limit_bytes=VMEM_LIMIT),
        cost_estimate=pl.CostEstimate(flops=flops, bytes_accessed=moved, transcendentals=0),
        name=name,
    )(scalars, *operands)


def bf16(*shape):
    return jax.ShapeDtypeStruct(shape, BF16)


def payload(group, down, up, n):
    owned, rank, width = down.shape
    slab, part = up.shape[2], width // 2
    specs = [
        pl.BlockSpec((owned, rank, part), lambda i, s: (0, 0, s[0])),
        pl.BlockSpec((owned, rank, slab), lambda i, s: (0, 0, 0)),
    ]
    shape = bf16(n * owned, rank, part + slab)
    return call(payload_kernel, "payload", shape, group[None], [down, up], specs)


def project(group, slab_index, slots, x, weighted, received, other):
    rows, width = x.shape
    tenants, rank, part = other.shape
    slab = received.shape[2] - part
    blocks = slots.shape[0]
    whole = lambda i, s: (0, 0, 0)
    specs = [
        pl.BlockSpec((rows, width), lambda i, s: (0, 0)),
        pl.BlockSpec((rows, slab), lambda i, s: (0, s[blocks + 1])),
        pl.BlockSpec((tenants, rank, part), whole),
        pl.BlockSpec((tenants, rank, part), whole),
        pl.BlockSpec((tenants, rank, slab), lambda i, s: (0, 0, part // slab)),
    ]
    return call(
        functools.partial(project_kernel, blocks),
        "project",
        bf16(rows, 2 * rank),
        jnp.stack([*slots, group, slab_index]),
        [x, weighted, received, other, received],
        specs,
        flops=2 * rows * rank * (width + slab),
        moved=2 * (rows + tenants * rank) * (width + slab),
    )


def adapter_grads(slab_index, slots, x, weighted, here, there, tenants, slab):
    rows, width = x.shape
    rank = here.shape[1] // 2
    blocks = slots.shape[0]
    ranks = pl.BlockSpec((rows, 2 * rank), lambda i, s: (0, 0))
    specs = [
        pl.BlockSpec((rows, width), lambda i, s: (0, 0)),
        pl.BlockSpec((rows, slab), lambda i, s: (0, s[blocks])),
        ranks,
        ranks,
    ]
    return call(
        functools.partial(grads_kernel, blocks),
        "adapter_grads",
        (bf16(tenants, rank, width + slab), bf16(rows, rank)),
        jnp.stack([*slots, slab_index]),
        [x, weighted, here, there],
        specs,
        scratch=[pltpu.VMEM((tenants, rank, width + slab), F32)],
        flops=2 * rows * rank * (width + slab),
        moved=2 * (rows + tenants * rank) * (width + slab),
    )


def owner_sums(got, n, width):
    tenants, rank, both = got.shape
    owned = tenants // n
    return pl.pallas_call(
        sum_kernel,
        out_shape=(
            jax.ShapeDtypeStruct((owned, rank, width), F32),
            jax.ShapeDtypeStruct((owned, rank, both - width), F32),
        ),
        compiler_params=pltpu.CompilerParams(vmem_limit_bytes=VMEM_LIMIT),
        cost_estimate=pl.CostEstimate(
            flops=got.size, bytes_accessed=2 * got.size, transcendentals=0
        ),
        name="owner_sums",
    )(got)


def edge_pairs(parity, k, n):
    pairs = []
    for i in range(parity, n - 1, 2):
        if i >= k - 1:
            pairs.append((i, i + 1))
        if i + 1 <= n - k:
            pairs.append((i + 1, i))
    return pairs


def swap_pairs(pairs, n, groups):
    targets = [b for _, b in pairs]
    return [(g * n + t, (groups - 1 - g) * n + t) for g in range(groups) for t in targets]


def after(value, *others):
    return lax.optimization_barrier((value, others))[0]


def pair_sum(value):
    return (value.astype(F32) + rest_of(value, "pipe")).astype(BF16)


def rest_of(value, axis):
    size = lax.axis_size(axis)
    rest = 0.0
    for d in range(1, size):
        pairs = [(i, (i + d) % size) for i in range(size)]
        with jax.named_scope(f"psum_{axis}"):
            rest = rest + lax.ppermute(value, axis, pairs).astype(F32)
    return rest


def per_device(
    sizes,
    layer_input,
    out_grad,
    value_weight,
    adapter_down,
    adapter_up,
    block_tenant,
    tenant_slot,
    forget_flag,
):
    n, groups = sizes
    token_rows, width = layer_input.shape
    rank = adapter_down.shape[1]
    slab = adapter_up.shape[2]
    tenants = tenant_slot.shape[0]
    depth = value_weight.shape[0]
    swap = lambda axis: functools.partial(lax.ppermute, axis_name=axis, perm=[(0, 1), (1, 0)])

    half = width // 2
    group = lax.axis_index("groups").astype(jnp.int32)
    me = lax.axis_index("seq").astype(jnp.int32)
    slab_index = lax.axis_index(("tensor", "pipe")).astype(jnp.int32)
    columns = lambda a: lax.dynamic_slice_in_dim(a, group * half, half, a.ndim - 1)

    with jax.named_scope("adapters"):
        received = lax.all_to_all(
            payload(group, adapter_down, adapter_up, n),
            "seq",
            split_axis=0,
            concat_axis=0,
            tiled=True,
        )
    with jax.named_scope("swap_a"):
        down_other = swap("groups")(received[:, :, :half])

    row_sign = (1 - 2 * forget_flag).astype(BF16)
    weighted = out_grad * row_sign[:, None]
    tenant_ids = jnp.arange(tenants, dtype=jnp.int32)
    slots = jnp.sum(
        jnp.where(block_tenant == tenant_ids[None, :], tenant_slot[None, :], 0), axis=1
    ).astype(jnp.int32)

    depth = value_weight.shape[0]
    arrived, begins, pairs_of = [], [me * depth], []

    def advance(k, last, *before):
        last, new = after(last, before), [None, None]
        for parity in (0, 1):
            pairs = edge_pairs(parity, k, n)
            if not pairs:
                continue
            owner = jnp.where(me % 2 != parity, me - k, me + k)
            cuts = 2 if k == n - 1 else 1
            for c in range(cuts):
                span = slice(c * depth // cuts, (c + 1) * depth // cuts)
                with jax.named_scope(f"line_{k}_{parity}_{c}"):
                    new[parity] = lax.ppermute(last[1 - parity][span], "seq", pairs)
                arrived.append(new[parity])
                pairs_of.append(pairs)
                begins.append(
                    jnp.where((owner >= 0) & (owner < n), owner * depth + span.start, -1)
                )
        return new

    def exchange(j, *before):
        with jax.named_scope(f"swap_w_{j}"):
            return lax.ppermute(
                after(arrived[j], before), ("groups", "seq"), swap_pairs(pairs_of[j], n, groups)
            )

    last = advance(1, [columns(value_weight)] * 2)
    for k in range(2, n - 1):
        last = advance(k, last, received)
    with jax.named_scope("ranks"):
        part = project(group, slab_index, slots, layer_input, weighted, received, down_other)
        here = pair_sum(part)
        there = rest_of(here, "tensor").astype(BF16)
        swapped = [None] * (len(arrived) + 2)
        swapped[0] = exchange(0, down_other)
        table, low_b = adapter_grads(
            slab_index, slots, layer_input, weighted, here, there, tenants, slab
        )
        advance(n - 1, last, table, swapped[0])
        swapped = swapped[: len(arrived)]
        got = lax.all_to_all(table, "seq", split_axis=0, concat_axis=0, tiled=True)
    for j in range(len(arrived)):
        if swapped[j] is None:
            swapped[j] = exchange(j, *([table] if j in (1, 2, 3) else []))

    common = (slots, begins, weighted, low_b)
    first = product(group, *common, received, value_weight, arrived)
    full = product(1 - group, *common, down_other, value_weight, swapped, first)
    down_grad, up_grad = owner_sums(got, n, width)
    return full, down_grad, up_grad


def solution(mesh):
    sizes = (mesh.shape["seq"], mesh.shape["groups"])
    return jax.shard_map(
        functools.partial(per_device, sizes),
        mesh=mesh,
        in_specs=(
            P(("groups", "seq"), ("tensor", "pipe")),
            P(("groups", "seq"), None),
            P("seq", ("tensor", "pipe")),
            P("seq", None, ("tensor", "pipe")),
            P("seq", None, ("tensor", "pipe")),
            P(("groups", "seq"), None),
            P(),
            P(("groups", "seq")),
        ),
        out_specs=(
            P(("groups", "seq"), ("tensor", "pipe")),
            P(("groups", "seq"), None, ("tensor", "pipe")),
            P(("groups", "seq"), None, ("tensor", "pipe")),
        ),
        check_vma=False,
    )
```

```python
import functools

import jax
import jax.numpy as jnp
from jax import lax
from jax.experimental import pallas as pl
from jax.experimental.pallas import tpu as pltpu
from jax.sharding import PartitionSpec as P

SCALE = 2.0
VMEM_LIMIT = 48 << 20
F32 = jnp.float32
BF16 = jnp.bfloat16


ROWS_BY_ROWS = (((1,), (1,)), ((), ()))
COLUMNS_BY_COLUMNS = (((0,), (0,)), ((), ()))


def payload_kernel(scalars, down_ref, up_ref, out_ref):
    owned, _, part = down_ref.shape
    for k in range(out_ref.shape[0] // owned):
        span = slice(k * owned, (k + 1) * owned)
        out_ref[span, :, :part] = down_ref[...]
        out_ref[span, :, part:] = up_ref[...]


def project_kernel(blocks, part, scalars, x_ref, w_ref, mine_ref, other_ref, out_ref):
    rows = x_ref.shape[0] // blocks
    rank, cut = mine_ref.shape[1], mine_ref.shape[2] - part

    def over(a, b):
        return lax.dot_general(a, b, ROWS_BY_ROWS, preferred_element_type=F32)

    def run(first, second):
        for b in range(blocks):
            s = scalars[b]
            span = slice(b * rows, (b + 1) * rows)
            hidden = over(x_ref[span, :part], first[s, :, :part])
            hidden += over(x_ref[span, part:], second[s, :, :part])
            low = over(w_ref[span, :cut], first[s, :, part:])
            if cut < w_ref.shape[1]:
                low += over(w_ref[span, cut:], second[s, :, part:])
            out_ref[span, :rank] = hidden.astype(BF16)
            out_ref[span, rank:] = low.astype(BF16)

    @pl.when(scalars[blocks] == 0)
    def _():
        run(mine_ref, other_ref)

    @pl.when(scalars[blocks] != 0)
    def _():
        run(other_ref, mine_ref)


def grads_kernel(blocks, scalars, x_ref, w_ref, here_ref, there_ref, table_ref, low_ref, acc_ref):
    rows, width = x_ref.shape[0] // blocks, x_ref.shape[1]
    rank = low_ref.shape[1]
    total = here_ref[...].astype(F32) + there_ref[...].astype(F32)
    hidden_b = total[:, :rank].astype(BF16)
    low_b = (SCALE * total[:, rank:]).astype(BF16)
    low_ref[...] = low_b
    acc_ref[...] = jnp.zeros_like(acc_ref)
    for b in range(blocks):
        s = scalars[b]
        span = slice(b * rows, (b + 1) * rows)
        acc_ref[s, :, :width] += lax.dot_general(
            low_b[span], x_ref[span, :], COLUMNS_BY_COLUMNS, preferred_element_type=F32
        )
        acc_ref[s, :, width:] += SCALE * lax.dot_general(
            hidden_b[span], w_ref[span, :], COLUMNS_BY_COLUMNS, preferred_element_type=F32
        )
    table_ref[...] = acc_ref[...].astype(BF16)


def sum_kernel(got_ref, down_ref, up_ref):
    count = got_ref.shape[0] // down_ref.shape[0]
    owned, _, width = down_ref.shape
    total = got_ref[:owned].astype(F32)
    for k in range(1, count):
        total += got_ref[k * owned : (k + 1) * owned].astype(F32)
    down_ref[...] = total[:, :, :width]
    up_ref[...] = total[:, :, width:]


def product_kernel(
    blocks, tiles, scalars, weighted_ref, low_ref, down_ref, own_ref, *refs
):
    out_ref, whole_ref, sems = refs[-3:]
    part = whole_ref.shape[1]
    tile = part // tiles
    pieces = refs[: scalars.shape[0] - blocks - 2]
    half = scalars[blocks]
    rows = weighted_ref.shape[0] // blocks

    def each(t, act):
        columns = pl.ds(t * tile, tile)
        own_columns = pl.ds(pl.multiple_of(half * part + t * tile, 128), tile)
        for j, source in enumerate([own_ref.at[:, own_columns]] + [p.at[:, columns] for p in pieces]):
            begin = scalars[blocks + 1 + j]

            def run(j=j, source=source, begin=begin):
                place = pl.ds(pl.multiple_of(begin, 16), source.shape[0])
                copy = pltpu.make_async_copy(source, whole_ref.at[place, columns], sems.at[t, j])
                copy.start() if act == "start" else copy.wait()

            if j:
                pl.when(begin >= 0)(run)
            else:
                run()

    for t in range(tiles):
        each(t, "start")
    for t in range(tiles):
        each(t, "wait")
        columns = slice(t * tile, (t + 1) * tile)
        total = jnp.dot(weighted_ref[...], whole_ref[:, columns], preferred_element_type=F32)
        for b in range(blocks):
            span = slice(b * rows, (b + 1) * rows)
            term = jnp.dot(
                low_ref[span, :], down_ref[scalars[b], :, columns], preferred_element_type=F32
            )
            out_ref[span, columns] = (total[span] + term).astype(BF16)


def product(half, slots, begins, weighted, low_b, down, own, pieces, into=None):
    rows = weighted.shape[0]
    width = own.shape[1]
    part = width // 2
    tiles = 2 if part % 256 == 0 else 1
    blocks = slots.shape[0]
    whole = lambda i, s: (0, 0)
    specs = [
        pl.BlockSpec(weighted.shape, whole),
        pl.BlockSpec(low_b.shape, whole),
        pl.BlockSpec((*down.shape[:2], part), lambda i, s: (0, 0, 0)),
    ] + [pl.BlockSpec(memory_space=pl.ANY) for _ in [own, *pieces]]
    operands = [weighted, low_b, down, own, *pieces]
    aliases = {}
    if into is not None:
        specs.append(pl.BlockSpec(memory_space=pl.ANY))
        operands.append(into)
        aliases = {len(operands): 0}
    return pl.pallas_call(
        functools.partial(product_kernel, blocks, tiles),
        out_shape=bf16(rows, width),
        grid_spec=pltpu.PrefetchScalarGridSpec(
            num_scalar_prefetch=1,
            grid=(1,),
            in_specs=specs,
            out_specs=pl.BlockSpec((rows, part), lambda i, s: (0, s[blocks])),
            scratch_shapes=[
                pltpu.VMEM((weighted.shape[1], part), BF16),
                pltpu.SemaphoreType.DMA((tiles, len(pieces) + 1)),
            ],
        ),
        input_output_aliases=aliases,
        compiler_params=pltpu.CompilerParams(vmem_limit_bytes=VMEM_LIMIT),
        cost_estimate=pl.CostEstimate(
            flops=24 * rows * part * weighted.shape[1],
            bytes_accessed=2 * part * (weighted.shape[1] + rows),
            transcendentals=0,
        ),
        name="product",
    )(jnp.stack([*slots, half, *begins]), *operands)


def call(kernel, name, out_shape, scalars, operands, specs=None, scratch=(), flops=0, moved=0, limit=VMEM_LIMIT):
    whole = lambda shape: pl.BlockSpec(shape, lambda i, s: (0,) * len(shape))
    specs = specs or [whole(o.shape) for o in operands]
    single = isinstance(out_shape, jax.ShapeDtypeStruct)
    return pl.pallas_call(
        kernel,
        out_shape=out_shape,
        grid_spec=pltpu.PrefetchScalarGridSpec(
            num_scalar_prefetch=1,
            grid=(1,),
            in_specs=specs,
            out_specs=whole(out_shape.shape) if single else [whole(o.shape) for o in out_shape],
            scratch_shapes=list(scratch),
        ),
        compiler_params=pltpu.CompilerParams(vmem_limit_bytes=limit),
        cost_estimate=pl.CostEstimate(flops=flops, bytes_accessed=moved, transcendentals=0),
        name=name,
    )(scalars, *operands)


def bf16(*shape):
    return jax.ShapeDtypeStruct(shape, BF16)


def payload(group, down, up, n):
    owned, rank, width = down.shape
    slab, part = up.shape[2], width // 2
    cut = slab // 2 if slab % 256 == 0 else slab
    specs = [
        pl.BlockSpec((owned, rank, part), lambda i, s: (0, 0, s[0])),
        pl.BlockSpec((owned, rank, cut), lambda i, s: (0, 0, s[0] if cut < slab else 0)),
    ]
    shape = bf16(n * owned, rank, part + cut)
    return call(
        payload_kernel, "payload", shape, group[None], [down, up], specs, limit=62 << 20
    )


def project(group, slab_index, slots, x, weighted, mine, other, slab):
    rows, width = x.shape
    rank = mine.shape[1]
    blocks = slots.shape[0]
    specs = [
        pl.BlockSpec((rows, width), lambda i, s: (0, 0)),
        pl.BlockSpec((rows, slab), lambda i, s: (0, s[blocks + 1])),
        pl.BlockSpec(mine.shape, lambda i, s: (0, 0, 0)),
        pl.BlockSpec(mine.shape, lambda i, s: (0, 0, 0)),
    ]
    return call(
        functools.partial(project_kernel, blocks, width // 2),
        "project",
        bf16(rows, 2 * rank),
        jnp.stack([*slots, group, slab_index]),
        [x, weighted, mine, other],
        specs,
        flops=2 * rows * rank * (width + slab),
        moved=2 * (rows * (width + slab) + 2 * mine.size),
    )


def adapter_grads(slab_index, slots, x, weighted, here, there, tenants, slab):
    rows, width = x.shape
    rank = here.shape[1] // 2
    blocks = slots.shape[0]
    ranks = pl.BlockSpec((rows, 2 * rank), lambda i, s: (0, 0))
    specs = [
        pl.BlockSpec((rows, width), lambda i, s: (0, 0)),
        pl.BlockSpec((rows, slab), lambda i, s: (0, s[blocks])),
        ranks,
        ranks,
    ]
    return call(
        functools.partial(grads_kernel, blocks),
        "adapter_grads",
        (bf16(tenants, rank, width + slab), bf16(rows, rank)),
        jnp.stack([*slots, slab_index]),
        [x, weighted, here, there],
        specs,
        scratch=[pltpu.VMEM((tenants, rank, width + slab), F32)],
        flops=2 * rows * rank * (width + slab),
        moved=2 * (rows + tenants * rank) * (width + slab),
    )


def owner_sums(got, n, width):
    tenants, rank, both = got.shape
    owned = tenants // n
    return pl.pallas_call(
        sum_kernel,
        out_shape=(
            jax.ShapeDtypeStruct((owned, rank, width), F32),
            jax.ShapeDtypeStruct((owned, rank, both - width), F32),
        ),
        compiler_params=pltpu.CompilerParams(vmem_limit_bytes=VMEM_LIMIT),
        cost_estimate=pl.CostEstimate(
            flops=got.size, bytes_accessed=2 * got.size, transcendentals=0
        ),
        name="owner_sums",
    )(got)


def edge_pairs(parity, k, n):
    pairs = []
    for i in range(parity, n - 1, 2):
        if i >= k - 1:
            pairs.append((i, i + 1))
        if i + 1 <= n - k:
            pairs.append((i + 1, i))
    return pairs


def swap_pairs(pairs, n, groups):
    targets = [b for _, b in pairs]
    return [(g * n + t, (groups - 1 - g) * n + t) for g in range(groups) for t in targets]


def after(value, *others):
    return lax.optimization_barrier((value, others))[0]


def pair_sum(value):
    return (value.astype(F32) + rest_of(value, "pipe")).astype(BF16)


def rest_of(value, axis):
    size = lax.axis_size(axis)
    rest = 0.0
    for d in range(1, size):
        pairs = [(i, (i + d) % size) for i in range(size)]
        with jax.named_scope(f"psum_{axis}"):
            rest = rest + lax.ppermute(value, axis, pairs).astype(F32)
    return rest


def per_device(
    sizes,
    layer_input,
    out_grad,
    value_weight,
    adapter_down,
    adapter_up,
    block_tenant,
    tenant_slot,
    forget_flag,
):
    n, groups = sizes
    token_rows, width = layer_input.shape
    rank = adapter_down.shape[1]
    slab = adapter_up.shape[2]
    tenants = tenant_slot.shape[0]
    depth = value_weight.shape[0]
    swap = lambda axis: functools.partial(lax.ppermute, axis_name=axis, perm=[(0, 1), (1, 0)])

    half = width // 2
    group = lax.axis_index("groups").astype(jnp.int32)
    me = lax.axis_index("seq").astype(jnp.int32)
    slab_index = lax.axis_index(("tensor", "pipe")).astype(jnp.int32)
    columns = lambda a: lax.dynamic_slice_in_dim(a, group * half, half, a.ndim - 1)

    with jax.named_scope("adapters"):
        received = lax.all_to_all(
            payload(group, adapter_down, adapter_up, n),
            "seq",
            split_axis=0,
            concat_axis=0,
            tiled=True,
        )
    with jax.named_scope("swap_a"):
        down_other = swap("groups")(received)

    row_sign = (1 - 2 * forget_flag).astype(BF16)
    weighted = out_grad * row_sign[:, None]
    tenant_ids = jnp.arange(tenants, dtype=jnp.int32)
    slots = jnp.sum(
        jnp.where(block_tenant == tenant_ids[None, :], tenant_slot[None, :], 0), axis=1
    ).astype(jnp.int32)

    depth = value_weight.shape[0]
    arrived, begins, pairs_of = [], [me * depth], []

    def advance(k, last, *before):
        last, new = after(last, before), [None, None]
        for parity in (0, 1):
            pairs = edge_pairs(parity, k, n)
            if not pairs:
                continue
            owner = jnp.where(me % 2 != parity, me - k, me + k)
            cuts = 2 if k == n - 1 else 1
            for c in range(cuts):
                span = slice(c * depth // cuts, (c + 1) * depth // cuts)
                with jax.named_scope(f"line_{k}_{parity}_{c}"):
                    new[parity] = lax.ppermute(last[1 - parity][span], "seq", pairs)
                arrived.append(new[parity])
                pairs_of.append(pairs)
                begins.append(
                    jnp.where((owner >= 0) & (owner < n), owner * depth + span.start, -1)
                )
        return new

    def exchange(j, *before):
        with jax.named_scope(f"swap_w_{j}"):
            return lax.ppermute(
                after(arrived[j], before), ("groups", "seq"), swap_pairs(pairs_of[j], n, groups)
            )

    last = advance(1, [columns(value_weight)] * 2)
    for k in range(2, n - 1):
        last = advance(k, last, received)
    with jax.named_scope("ranks"):
        part = project(
            group, slab_index, slots, layer_input, weighted, received, down_other, slab
        )
        here = pair_sum(part)
        there = rest_of(here, "tensor").astype(BF16)
        swapped = [None] * (len(arrived) + 2)
        swapped[0] = exchange(0, down_other)
        table, low_b = adapter_grads(
            slab_index, slots, layer_input, weighted, here, there, tenants, slab
        )
        advance(n - 1, last, table, swapped[0])
        swapped = swapped[: len(arrived)]
        got = lax.all_to_all(table, "seq", split_axis=0, concat_axis=0, tiled=True)
    for j in range(len(arrived)):
        if swapped[j] is None:
            swapped[j] = exchange(j, *([table] if j in (1, 2, 3) else []))

    common = (slots, begins, weighted, low_b)
    first = product(group, *common, received, value_weight, arrived)
    full = product(1 - group, *common, down_other, value_weight, swapped, first)
    down_grad, up_grad = owner_sums(got, n, width)
    return full, down_grad, up_grad


def solution(mesh):
    sizes = (mesh.shape["seq"], mesh.shape["groups"])
    return jax.shard_map(
        functools.partial(per_device, sizes),
        mesh=mesh,
        in_specs=(
            P(("groups", "seq"), ("tensor", "pipe")),
            P(("groups", "seq"), None),
            P("seq", ("tensor", "pipe")),
            P("seq", None, ("tensor", "pipe")),
            P("seq", None, ("tensor", "pipe")),
            P(("groups", "seq"), None),
            P(),
            P(("groups", "seq")),
        ),
        out_specs=(
            P(("groups", "seq"), ("tensor", "pipe")),
            P(("groups", "seq"), None, ("tensor", "pipe")),
            P(("groups", "seq"), None, ("tensor", "pipe")),
        ),
        check_vma=False,
    )
```

```python
import functools

import jax
import jax.numpy as jnp
from jax import lax
from jax.experimental import pallas as pl
from jax.experimental.pallas import tpu as pltpu
from jax.sharding import PartitionSpec as P

SCALE = 2.0
VMEM_LIMIT = 48 << 20
F32 = jnp.float32
BF16 = jnp.bfloat16


ROWS_BY_ROWS = (((1,), (1,)), ((), ()))
COLUMNS_BY_COLUMNS = (((0,), (0,)), ((), ()))


def payload_kernel(scalars, down_ref, up_ref, out_ref):
    owned, _, part = down_ref.shape
    for k in range(out_ref.shape[0] // owned):
        span = slice(k * owned, (k + 1) * owned)
        out_ref[span, :, :part] = down_ref[...]
        out_ref[span, :, part:] = up_ref[...]


def project_kernel(blocks, part, scalars, x_ref, w_ref, mine_ref, other_ref, out_ref):
    rows = x_ref.shape[0] // blocks
    rank, cut = mine_ref.shape[1], mine_ref.shape[2] - part

    def over(a, b):
        return lax.dot_general(a, b, ROWS_BY_ROWS, preferred_element_type=F32)

    def run(first, second):
        for b in range(blocks):
            s = scalars[b]
            span = slice(b * rows, (b + 1) * rows)
            hidden = over(x_ref[span, :part], first[s, :, :part])
            hidden += over(x_ref[span, part:], second[s, :, :part])
            low = over(w_ref[span, :cut], first[s, :, part:])
            if cut < w_ref.shape[1]:
                low += over(w_ref[span, cut:], second[s, :, part:])
            out_ref[span, :rank] = hidden.astype(BF16)
            out_ref[span, rank:] = low.astype(BF16)

    @pl.when(scalars[blocks] == 0)
    def _():
        run(mine_ref, other_ref)

    @pl.when(scalars[blocks] != 0)
    def _():
        run(other_ref, mine_ref)


def grads_kernel(blocks, scalars, x_ref, w_ref, here_ref, there_ref, table_ref, low_ref, acc_ref):
    rows, width = x_ref.shape[0] // blocks, x_ref.shape[1]
    rank = low_ref.shape[1]
    total = here_ref[...].astype(F32) + there_ref[...].astype(F32)
    hidden_b = total[:, :rank].astype(BF16)
    low_b = (SCALE * total[:, rank:]).astype(BF16)
    low_ref[...] = low_b
    acc_ref[...] = jnp.zeros_like(acc_ref)
    for b in range(blocks):
        s = scalars[b]
        span = slice(b * rows, (b + 1) * rows)
        acc_ref[s, :, :width] += lax.dot_general(
            low_b[span], x_ref[span, :], COLUMNS_BY_COLUMNS, preferred_element_type=F32
        )
        acc_ref[s, :, width:] += SCALE * lax.dot_general(
            hidden_b[span], w_ref[span, :], COLUMNS_BY_COLUMNS, preferred_element_type=F32
        )
    table_ref[...] = acc_ref[...].astype(BF16)


def sum_kernel(got_ref, down_ref, up_ref):
    count = got_ref.shape[0] // down_ref.shape[0]
    owned, _, width = down_ref.shape
    total = got_ref[:owned].astype(F32)
    for k in range(1, count):
        total += got_ref[k * owned : (k + 1) * owned].astype(F32)
    down_ref[...] = total[:, :, :width]
    up_ref[...] = total[:, :, width:]


def product_kernel(
    blocks, tiles, scalars, weighted_ref, low_ref, down_ref, own_ref, *refs
):
    out_ref, whole_ref, sems = refs[-3:]
    part = whole_ref.shape[1]
    tile = part // tiles
    pieces = refs[: scalars.shape[0] - blocks - 2]
    half = scalars[blocks]
    rows = weighted_ref.shape[0] // blocks

    def each(t, act):
        columns = pl.ds(t * tile, tile)
        own_columns = pl.ds(pl.multiple_of(half * part + t * tile, 128), tile)
        for j, source in enumerate([own_ref.at[:, own_columns]] + [p.at[:, columns] for p in pieces]):
            begin = scalars[blocks + 1 + j]

            def run(j=j, source=source, begin=begin):
                place = pl.ds(pl.multiple_of(begin, 16), source.shape[0])
                copy = pltpu.make_async_copy(source, whole_ref.at[place, columns], sems.at[t, j])
                copy.start() if act == "start" else copy.wait()

            if j:
                pl.when(begin >= 0)(run)
            else:
                run()

    for t in range(tiles):
        each(t, "start")
    for t in range(tiles):
        each(t, "wait")
        columns = slice(t * tile, (t + 1) * tile)
        total = jnp.dot(weighted_ref[...], whole_ref[:, columns], preferred_element_type=F32)
        for b in range(blocks):
            span = slice(b * rows, (b + 1) * rows)
            term = jnp.dot(
                low_ref[span, :], down_ref[scalars[b], :, columns], preferred_element_type=F32
            )
            out_ref[span, columns] = (total[span] + term).astype(BF16)


def product(half, slots, begins, weighted, low_b, down, own, pieces, into=None):
    rows = weighted.shape[0]
    width = own.shape[1]
    part = width // 2
    tiles = 2 if part % 256 == 0 else 1
    blocks = slots.shape[0]
    whole = lambda i, s: (0, 0)
    specs = [
        pl.BlockSpec(weighted.shape, whole),
        pl.BlockSpec(low_b.shape, whole),
        pl.BlockSpec((*down.shape[:2], part), lambda i, s: (0, 0, 0)),
    ] + [pl.BlockSpec(memory_space=pl.ANY) for _ in [own, *pieces]]
    operands = [weighted, low_b, down, own, *pieces]
    aliases = {}
    if into is not None:
        specs.append(pl.BlockSpec(memory_space=pl.ANY))
        operands.append(into)
        aliases = {len(operands): 0}
    return pl.pallas_call(
        functools.partial(product_kernel, blocks, tiles),
        out_shape=bf16(rows, width),
        grid_spec=pltpu.PrefetchScalarGridSpec(
            num_scalar_prefetch=1,
            grid=(1,),
            in_specs=specs,
            out_specs=pl.BlockSpec((rows, part), lambda i, s: (0, s[blocks])),
            scratch_shapes=[
                pltpu.VMEM((weighted.shape[1], part), BF16),
                pltpu.SemaphoreType.DMA((tiles, len(pieces) + 1)),
            ],
        ),
        input_output_aliases=aliases,
        compiler_params=pltpu.CompilerParams(vmem_limit_bytes=VMEM_LIMIT),
        cost_estimate=pl.CostEstimate(
            flops=24 * rows * part * weighted.shape[1],
            bytes_accessed=2 * part * (weighted.shape[1] + rows),
            transcendentals=0,
        ),
        name="product",
    )(jnp.stack([*slots, half, *begins]), *operands)


def call(kernel, name, out_shape, scalars, operands, specs=None, scratch=(), flops=0, moved=0, limit=VMEM_LIMIT):
    whole = lambda shape: pl.BlockSpec(shape, lambda i, s: (0,) * len(shape))
    specs = specs or [whole(o.shape) for o in operands]
    single = isinstance(out_shape, jax.ShapeDtypeStruct)
    return pl.pallas_call(
        kernel,
        out_shape=out_shape,
        grid_spec=pltpu.PrefetchScalarGridSpec(
            num_scalar_prefetch=1,
            grid=(1,),
            in_specs=specs,
            out_specs=whole(out_shape.shape) if single else [whole(o.shape) for o in out_shape],
            scratch_shapes=list(scratch),
        ),
        compiler_params=pltpu.CompilerParams(vmem_limit_bytes=limit),
        cost_estimate=pl.CostEstimate(flops=flops, bytes_accessed=moved, transcendentals=0),
        name=name,
    )(scalars, *operands)


def bf16(*shape):
    return jax.ShapeDtypeStruct(shape, BF16)


def payload(group, down, up, n):
    owned, rank, width = down.shape
    slab, part = up.shape[2], width // 2
    cut = slab // 2 if slab % 256 == 0 else slab
    specs = [
        pl.BlockSpec((owned, rank, part), lambda i, s: (0, 0, s[0])),
        pl.BlockSpec((owned, rank, cut), lambda i, s: (0, 0, s[0] if cut < slab else 0)),
    ]
    shape = bf16(n * owned, rank, part + cut)
    return call(
        payload_kernel, "payload", shape, group[None], [down, up], specs, limit=62 << 20
    )


def project(group, slab_index, slots, x, weighted, mine, other, slab):
    rows, width = x.shape
    rank = mine.shape[1]
    blocks = slots.shape[0]
    specs = [
        pl.BlockSpec((rows, width), lambda i, s: (0, 0)),
        pl.BlockSpec((rows, slab), lambda i, s: (0, s[blocks + 1])),
        pl.BlockSpec(mine.shape, lambda i, s: (0, 0, 0)),
        pl.BlockSpec(mine.shape, lambda i, s: (0, 0, 0)),
    ]
    return call(
        functools.partial(project_kernel, blocks, width // 2),
        "project",
        bf16(rows, 2 * rank),
        jnp.stack([*slots, group, slab_index]),
        [x, weighted, mine, other],
        specs,
        flops=2 * rows * rank * (width + slab),
        moved=2 * (rows * (width + slab) + 2 * mine.size),
    )


def adapter_grads(slab_index, slots, x, weighted, here, there, tenants, slab):
    rows, width = x.shape
    rank = here.shape[1] // 2
    blocks = slots.shape[0]
    ranks = pl.BlockSpec((rows, 2 * rank), lambda i, s: (0, 0))
    specs = [
        pl.BlockSpec((rows, width), lambda i, s: (0, 0)),
        pl.BlockSpec((rows, slab), lambda i, s: (0, s[blocks])),
        ranks,
        ranks,
    ]
    return call(
        functools.partial(grads_kernel, blocks),
        "adapter_grads",
        (bf16(tenants, rank, width + slab), bf16(rows, rank)),
        jnp.stack([*slots, slab_index]),
        [x, weighted, here, there],
        specs,
        scratch=[pltpu.VMEM((tenants, rank, width + slab), F32)],
        flops=2 * rows * rank * (width + slab),
        moved=2 * (rows + tenants * rank) * (width + slab),
    )


def owner_sums(got, n, width):
    tenants, rank, both = got.shape
    owned = tenants // n
    return pl.pallas_call(
        sum_kernel,
        out_shape=(
            jax.ShapeDtypeStruct((owned, rank, width), F32),
            jax.ShapeDtypeStruct((owned, rank, both - width), F32),
        ),
        compiler_params=pltpu.CompilerParams(vmem_limit_bytes=VMEM_LIMIT),
        cost_estimate=pl.CostEstimate(
            flops=got.size, bytes_accessed=2 * got.size, transcendentals=0
        ),
        name="owner_sums",
    )(got)


def edge_pairs(parity, k, n):
    pairs = []
    for i in range(parity, n - 1, 2):
        if i >= k - 1:
            pairs.append((i, i + 1))
        if i + 1 <= n - k:
            pairs.append((i + 1, i))
    return pairs


def swap_pairs(pairs, n, groups):
    targets = [b for _, b in pairs]
    return [(g * n + t, (groups - 1 - g) * n + t) for g in range(groups) for t in targets]


def after(value, *others):
    return lax.optimization_barrier((value, others))[0]


def pair_sum(value):
    return (value.astype(F32) + rest_of(value, "pipe")).astype(BF16)


def rest_of(value, axis):
    size = lax.axis_size(axis)
    rest = 0.0
    for d in range(1, size):
        pairs = [(i, (i + d) % size) for i in range(size)]
        with jax.named_scope(f"psum_{axis}"):
            rest = rest + lax.ppermute(value, axis, pairs).astype(F32)
    return rest


def per_device(
    sizes,
    layer_input,
    out_grad,
    value_weight,
    adapter_down,
    adapter_up,
    block_tenant,
    tenant_slot,
    forget_flag,
):
    n, groups = sizes
    token_rows, width = layer_input.shape
    rank = adapter_down.shape[1]
    slab = adapter_up.shape[2]
    tenants = tenant_slot.shape[0]
    depth = value_weight.shape[0]
    swap = lambda axis: functools.partial(lax.ppermute, axis_name=axis, perm=[(0, 1), (1, 0)])

    half = width // 2
    group = lax.axis_index("groups").astype(jnp.int32)
    me = lax.axis_index("seq").astype(jnp.int32)
    slab_index = lax.axis_index(("tensor", "pipe")).astype(jnp.int32)
    columns = lambda a: lax.dynamic_slice_in_dim(a, group * half, half, a.ndim - 1)

    with jax.named_scope("adapters"):
        received = lax.all_to_all(
            payload(group, adapter_down, adapter_up, n),
            "seq",
            split_axis=0,
            concat_axis=0,
            tiled=True,
        )
    with jax.named_scope("swap_a"):
        down_other = swap("groups")(received)

    row_sign = (1 - 2 * forget_flag).astype(BF16)
    weighted = out_grad * row_sign[:, None]
    tenant_ids = jnp.arange(tenants, dtype=jnp.int32)
    slots = jnp.sum(
        jnp.where(block_tenant == tenant_ids[None, :], tenant_slot[None, :], 0), axis=1
    ).astype(jnp.int32)

    depth = value_weight.shape[0]
    arrived, begins, pairs_of = [], [me * depth], []

    def advance(k, last, *before):
        last, new = after(last, before), [None, None]
        for parity in (0, 1):
            pairs = edge_pairs(parity, k, n)
            if not pairs:
                continue
            owner = jnp.where(me % 2 != parity, me - k, me + k)
            cuts = 2 if k == n - 1 else 1
            for c in range(cuts):
                span = slice(c * depth // cuts, (c + 1) * depth // cuts)
                with jax.named_scope(f"line_{k}_{parity}_{c}"):
                    new[parity] = lax.ppermute(last[1 - parity][span], "seq", pairs)
                arrived.append(new[parity])
                pairs_of.append(pairs)
                begins.append(
                    jnp.where((owner >= 0) & (owner < n), owner * depth + span.start, -1)
                )
        return new

    def exchange(j, *before):
        with jax.named_scope(f"swap_w_{j}"):
            return lax.ppermute(
                after(arrived[j], before), ("groups", "seq"), swap_pairs(pairs_of[j], n, groups)
            )

    last = advance(1, [columns(value_weight)] * 2)
    for k in range(2, n - 1):
        last = advance(k, last, received)
    with jax.named_scope("ranks"):
        part = project(
            group, slab_index, slots, layer_input, weighted, received, down_other, slab
        )
        here = pair_sum(part)
        there = rest_of(here, "tensor").astype(BF16)
        swapped = [None] * (len(arrived) + 2)
        swapped[0] = exchange(0, down_other)
        table, low_b = adapter_grads(
            slab_index, slots, layer_input, weighted, here, there, tenants, slab
        )
        advance(n - 1, last, table, swapped[0])
        swapped = swapped[: len(arrived)]
        got = lax.all_to_all(table, "seq", split_axis=0, concat_axis=0, tiled=True)
    for j in range(len(arrived)):
        if swapped[j] is None:
            swapped[j] = exchange(j, *([table] if j in (2, 3) else [swapped[0]] if j == 1 else []))

    common = (slots, begins, weighted, low_b)
    first = product(group, *common, received, value_weight, arrived)
    full = product(1 - group, *common, down_other, value_weight, swapped, first)
    down_grad, up_grad = owner_sums(got, n, width)
    return full, down_grad, up_grad


def solution(mesh):
    sizes = (mesh.shape["seq"], mesh.shape["groups"])
    return jax.shard_map(
        functools.partial(per_device, sizes),
        mesh=mesh,
        in_specs=(
            P(("groups", "seq"), ("tensor", "pipe")),
            P(("groups", "seq"), None),
            P("seq", ("tensor", "pipe")),
            P("seq", None, ("tensor", "pipe")),
            P("seq", None, ("tensor", "pipe")),
            P(("groups", "seq"), None),
            P(),
            P(("groups", "seq")),
        ),
        out_specs=(
            P(("groups", "seq"), ("tensor", "pipe")),
            P(("groups", "seq"), None, ("tensor", "pipe")),
            P(("groups", "seq"), None, ("tensor", "pipe")),
        ),
        check_vma=False,
    )
```
